32 devices in a mesh: group: 2 (over y), samp: 4 (over z), band: 4 (over x, core).
Axes of the slice: x: 2, y: 2, z: 4, core: 2. Of those that a mesh axis runs over, the one named last changes fastest.
Arguments:
- features: bfloat16 [48, 8, 32, 256], P(None, ('group', 'samp'), 'band'), parts along dimension 1, may hold values from -6 to 6
- radiance: float32 [3, 8, 32, 256], P(None, ('group', 'samp'), 'band'), parts along dimension 1, may hold values from 0.02 to 16
- sample_order: int32 [8, 32, 32, 8], P(('group', 'samp'), 'band'), parts along dimension 0, may hold values from 0 to 7, each once within a row
- embed_first: bfloat16 [128, 48], replicated, may hold values from -0.875 to 0.875
- embed_second: bfloat16 [128, 128], replicated, may hold values from -0.5 to 0.5
- embed_third: bfloat16 [32, 128], replicated, may hold values from -0.5 to 0.5
- conv_first: bfloat16 [128, 800], replicated, may hold values from -0.21875 to 0.21875
- conv_second: bfloat16 [32, 128], replicated, may hold values from -0.5 to 0.5
- kernel_first: bfloat16 [128, 64], replicated, may hold values from -0.75 to 0.75
- kernel_second: bfloat16 [25, 128], replicated, may hold values from -0.5 to 0.5
Outputs:
- denoised: float32 [3, 64, 256], P(None, ('group', 'band'), 'samp'), parts along dimension 1
The draws below stay inside these ranges and needn't reach their ends.
There are 2 independent parts, one for each index of `group`. The reference program is written for one: setup_inputs(seed, part) draws one part's arguments, and reference() takes and returns one part's arrays. A program takes and returns all parts, laid end to end along the dimension named above; an argument that names none is the same for every part. Nothing has to cross between parts.
Inputs may be any that keep to these rules, and one draw needn't show every extreme that they name: `sample_order`: the 8 entries of each tile (the last dimension) are a permutation of 0 to 7; along a crop row each value appears once in every tile.
All inputs are finite; a program needn't handle non-finite values.
Results may differ from the reference program's by a relative error of at most 0.0003.
The reference program's roundings to bfloat16 on the way count: a program that leaves them out, or rounds other values in their place, can miss the bound.
Values may be sent and summed in bfloat16 or wider, within the bound.
A program may use at most 64 MiB of HBM per device.

```python
import math
import jax
import jax.numpy as jnp
from jax import lax

F_IN = 48
HID = 128
EMB = 32
CONV_HID = 128
KSIZE = 5
TILE = 8
W = 256
H = 32
SPP = 4


def shard_levels(stream_key, extent, shards, least, largest):
    level = 1.0
    for axis_at, parts in shards:
        steps = jax.random.uniform(jax.random.fold_in(jax.random.fold_in(stream_key, 6), axis_at), (parts,), jnp.float32, least / len(shards), largest / len(shards))
        level = level * jnp.repeat(jnp.exp(steps), extent[axis_at] // parts).reshape((-1,) + (1,) * (len(extent) - 1 - axis_at))
    return level


def gaussian(rng, shape, width, most, pieces=(), held_as=jnp.bfloat16):
    drawn = jax.random.normal(rng, shape, jnp.float32) * width
    if len(pieces) > 0:
        drawn = shard_levels(rng, shape, pieces, -0.22, 0.18) * drawn
    return jnp.clip(drawn, min=-most, max=most).astype(held_as)


def setup_inputs(seed: int = 0, part: int = 0) -> dict:
    key_list = jax.random.split(jax.random.key(seed), 11)
    own_keys = jax.random.split(jax.random.fold_in(key_list[10], part), 11)
    return {
        "features": gaussian(own_keys[0], (F_IN, SPP, H, W), 1.0, 6.0, ((1, 4), (2, 4))),
        "radiance": jnp.clip(jnp.exp(math.log(16.0) - 6.684612 * jax.random.uniform(own_keys[1], (3, SPP, H, W), jnp.float32) ** shard_levels(own_keys[1], (3, SPP, H, W), ((1, 4), (2, 4)), -0.2, 0.2)), 0.02, 16.0),
        "sample_order": jax.vmap(lambda own: jax.random.permutation(own, TILE))(jax.random.split(own_keys[2], SPP * H * (W // TILE))).reshape((SPP, H, W // TILE, TILE)).astype(jnp.int32),
        "embed_first": gaussian(key_list[3], (HID, F_IN), F_IN ** -0.5, 0.875),
        "embed_second": gaussian(key_list[4], (HID, HID), HID ** -0.5, 0.5),
        "embed_third": gaussian(key_list[5], (EMB, HID), HID ** -0.5, 0.5),
        "conv_first": gaussian(key_list[6], (CONV_HID, KSIZE * KSIZE * EMB), (KSIZE * KSIZE * EMB) ** -0.5, 0.21875),
        "conv_second": gaussian(key_list[7], (EMB, CONV_HID), CONV_HID ** -0.5, 0.5),
        "kernel_first": gaussian(key_list[8], (HID, 2 * EMB), (2 * EMB) ** -0.5, 0.75),
        "kernel_second": gaussian(key_list[9], (KSIZE * KSIZE, HID), HID ** -0.5, 0.5),
    }


def inverse_order(sample_order):
    slot_ids = jnp.arange(sample_order.shape[-1], dtype=jnp.int32)
    matches = (sample_order[..., :, None] == slot_ids).astype(jnp.int32)
    return lax.optimization_barrier(jnp.sum(matches * slot_ids[:, None], axis=-2)).astype(jnp.int32)

def to_pixels(values, inverse):
    shaped = values.reshape(values.shape[:-1] + (inverse.shape[-2], inverse.shape[-1]))
    picker = jnp.broadcast_to(inverse[None], shaped.shape)
    picked = jnp.take_along_axis(shaped, picker, axis=-1)
    return picked.reshape(values.shape)

def embed_samples(columns, embed_first, embed_second, embed_third):
    layer_one = jax.nn.relu(jnp.dot(embed_first, columns, preferred_element_type=jnp.float32)).astype(jnp.bfloat16)
    layer_two = jax.nn.relu(jnp.dot(embed_second, layer_one, preferred_element_type=jnp.float32)).astype(jnp.bfloat16)
    return jnp.dot(embed_third, layer_two, preferred_element_type=jnp.float32)

def convolve(padded, row_count, col_count, conv_first, conv_second):
    shifted = [padded[:, row_off:row_off + row_count, col_off:col_off + col_count] for row_off in range(KSIZE) for col_off in range(KSIZE)]
    stacked = jnp.stack(shifted).reshape(-1, row_count * col_count)
    hidden = jax.nn.relu(jnp.dot(conv_first, stacked, preferred_element_type=jnp.float32)).astype(jnp.bfloat16)
    result = jnp.dot(conv_second, hidden, preferred_element_type=jnp.float32).astype(jnp.bfloat16)
    return result.reshape(-1, row_count, col_count)

def reference(features, radiance, sample_order, embed_first, embed_second, embed_third, conv_first, conv_second, kernel_first, kernel_second):
    inverse = inverse_order(sample_order)
    ordered = to_pixels(features, inverse)
    lights = to_pixels(radiance, inverse)
    channels, per_pixel, height, crop_width = ordered.shape
    emb_width = embed_third.shape[0]
    radius = KSIZE // 2

    def one_sample(sample_plane):
        return embed_samples(sample_plane.reshape(channels, -1), embed_first, embed_second, embed_third).reshape(emb_width, height, crop_width)
    embedded = lax.map(one_sample, jnp.moveaxis(ordered, 1, 0))
    pooled = (lax.optimization_barrier(jnp.sum(embedded, axis=0)) * (1.0 / math.sqrt(per_pixel))).astype(jnp.bfloat16)
    padded = jnp.pad(pooled, ((0, 0), (radius, radius), (radius, radius)))
    context = convolve(padded, height, crop_width, conv_first, conv_second)
    ctx_part = jnp.dot(kernel_first[:, emb_width:], context.reshape(emb_width, -1), preferred_element_type=jnp.float32)

    def splat_one(canvas, sample_item):
        emb_plane, colour = sample_item
        emb_bf = emb_plane.astype(jnp.bfloat16).reshape(emb_width, -1)
        hidden = jax.nn.relu(jnp.dot(kernel_first[:, :emb_width], emb_bf, preferred_element_type=jnp.float32) + ctx_part).astype(jnp.bfloat16)
        weights = jnp.exp(jnp.dot(kernel_second, hidden, preferred_element_type=jnp.float32)).reshape(-1, height, crop_width)
        with_ones = jnp.concatenate([colour, jnp.ones((1, height, crop_width), jnp.float32)], axis=0)
        for row_off in range(KSIZE):
            for col_off in range(KSIZE):
                tap_index = row_off * KSIZE + col_off
                canvas = canvas.at[:, row_off:row_off + height, col_off:col_off + crop_width].add(weights[tap_index][None] * with_ones)
        return (canvas, None)
    start_canvas = jnp.zeros((4, height + 2 * radius, crop_width + 2 * radius), jnp.float32)
    canvas, unused = lax.scan(splat_one, start_canvas, (embedded, jnp.moveaxis(lights, 1, 0)))
    summed = canvas[:, radius:radius + height, radius:radius + crop_width]
    return summed[:3] / summed[3:4]
```

```python
import functools
import math

import jax
import jax.numpy as jnp
from jax import lax
from jax.experimental import pallas as pl
from jax.experimental.pallas import tpu as pltpu
from jax.sharding import PartitionSpec as P

KSIZE = 5
LANES = 128
SENT = jnp.bfloat16


def padded_2(cells, sides, width):
    for axis, dim in sides:
        count = lax.axis_size(axis)
        ends = count - 1
        head = lax.slice_in_dim(cells, 0, width, axis=dim)
        tail = lax.slice_in_dim(cells, cells.shape[dim] - width, cells.shape[dim], axis=dim)
        cells = jnp.concatenate(
            [
                lax.ppermute(tail, axis, [(i, (i + 1) % count) for i in range(ends)]),
                cells,
                lax.ppermute(head, axis, [((i + 1) % count, i) for i in range(ends)]),
            ],
            axis=dim,
        )
    return cells


def passed_along(block, axis, distance):
    devices = range(lax.axis_size(axis))
    route = [(i - distance, i) for i in devices if i - distance in devices]
    return lax.ppermute(block, axis, route)


def to_pixels(values, sample_order):
    tile_size = sample_order.shape[-1]
    dest_cols = sample_order.reshape(sample_order.shape[:-2] + (-1,))
    offsets = jnp.arange(dest_cols.shape[-1], dtype=jnp.int32) % tile_size
    result = jnp.zeros_like(values)
    for slot_id in range(tile_size):
        spread = jnp.repeat(values[..., slot_id::tile_size], tile_size, axis=-1)
        target = jnp.repeat(dest_cols[..., slot_id::tile_size], tile_size, axis=-1)
        result = jnp.where((target == offsets)[None], spread, result)
    return result


def embed_samples(columns, embed_first, embed_second, embed_third):
    layer_one = jax.nn.relu(
        jnp.dot(embed_first, columns, preferred_element_type=jnp.float32)
    ).astype(jnp.bfloat16)
    layer_two = jax.nn.relu(
        jnp.dot(embed_second, layer_one, preferred_element_type=jnp.float32)
    ).astype(jnp.bfloat16)
    return jnp.dot(embed_third, layer_two, preferred_element_type=jnp.float32)


def convolve(padded, row_count, col_count, conv_first, conv_second):
    shifted = [
        padded[:, row_off : row_off + row_count, col_off : col_off + col_count]
        for row_off in range(KSIZE)
        for col_off in range(KSIZE)
    ]
    stacked = jnp.stack(shifted).reshape(-1, row_count * col_count)
    hidden = jax.nn.relu(jnp.dot(conv_first, stacked, preferred_element_type=jnp.float32)).astype(
        jnp.bfloat16
    )
    result = jnp.dot(conv_second, hidden, preferred_element_type=jnp.float32).astype(jnp.bfloat16)
    return result.reshape(-1, row_count, col_count)


def shards(
    features,
    radiance,
    sample_order,
    embed_first,
    embed_second,
    embed_third,
    conv_first,
    conv_second,
    kernel_first,
    kernel_second,
):
    ordered = to_pixels(features, sample_order)
    lights = to_pixels(radiance, sample_order)
    channels, samples_dev, row_count, crop_width = ordered.shape
    emb_width = embed_third.shape[0]
    radius = KSIZE // 2
    scaling = 1.0 / math.sqrt(samples_dev * lax.axis_size("samp"))
    embedded = embed_samples(ordered.reshape(channels, -1), embed_first, embed_second, embed_third)
    emb_bf = embedded.astype(jnp.bfloat16)
    own_part = jnp.dot(kernel_first[:, :emb_width], emb_bf, preferred_element_type=jnp.float32)
    own_part = own_part.reshape(-1, samples_dev, row_count, crop_width)
    partial_value = jnp.sum(embedded.reshape(emb_width, samples_dev, row_count, crop_width), axis=1)
    summed_emb = lax.psum(partial_value, "samp")
    pooled = (summed_emb * scaling).astype(jnp.bfloat16)
    padded = padded_2(pooled, (("band", 1),), 2)
    padded = jnp.pad(padded, ((0, 0), (0, 0), (radius, radius)))
    context = convolve(padded, row_count, crop_width, conv_first, conv_second)
    col_count = context.shape[2]
    ctx_part = jnp.dot(
        kernel_first[:, emb_width:],
        context.reshape(emb_width, -1),
        preferred_element_type=jnp.float32,
    )
    ctx_part = ctx_part.reshape(-1, 1, row_count, col_count)
    hidden = jax.nn.relu(own_part + ctx_part).astype(jnp.bfloat16)
    logits = jnp.dot(
        kernel_second, hidden.reshape(hidden.shape[0], -1), preferred_element_type=jnp.float32
    )
    weights = jnp.exp(logits).reshape(-1, samples_dev, row_count, col_count)
    with_ones = jnp.concatenate(
        [lights, jnp.ones((1, samples_dev, row_count, crop_width), jnp.float32)], axis=0
    )
    canvas = jnp.zeros((4, row_count + 2 * radius, crop_width + 2 * radius), jnp.float32)
    for row_off in range(KSIZE):
        for col_off in range(KSIZE):
            tap_index = row_off * KSIZE + col_off
            contrib = jnp.sum(weights[tap_index][None] * with_ones, axis=1)
            canvas = canvas.at[
                :, row_off : row_off + row_count, col_off : col_off + crop_width
            ].add(contrib)
    canvas = canvas[:, :, radius : radius + crop_width]
    summed_all = lax.psum_scatter(canvas, "samp", scatter_dimension=2, tiled=True)
    top_rims = summed_all[:, :radius]
    low_rims = summed_all[:, radius + row_count :]
    summed = summed_all[:, radius : radius + row_count]
    from_below = passed_along(top_rims, "band", -1)
    from_above = passed_along(low_rims, "band", 1)
    summed = summed.at[:, row_count - radius :].add(from_below)
    summed = summed.at[:, :radius].add(from_above)
    return summed[:3] / summed[3:4]


MESH = pl.DeviceIdType.MESH


def slots_to_sources(order, tile_size, width):
    rows, tiles, _ = order.shape
    flat = order.reshape(rows * tiles, tile_size).astype(jnp.float32).astype(jnp.bfloat16)
    slot = lax.broadcasted_iota(jnp.int32, (tile_size, width), 0)
    col = lax.broadcasted_iota(jnp.int32, (tile_size, width), 1)
    spread = jnp.where(slot == col % tile_size, 1.0, 0.0).astype(jnp.bfloat16)
    wide = jnp.dot(flat, spread, preferred_element_type=jnp.float32)
    tile_id = lax.broadcasted_iota(jnp.int32, (rows * tiles, width), 0) % tiles
    tile_of = lax.broadcasted_iota(jnp.int32, (rows * tiles, width), 1) // tile_size
    wide = jnp.where(tile_id == tile_of, wide, 0.0)
    dest = jnp.sum(wide.reshape(rows, tiles, width), axis=1).astype(jnp.int32)
    col = lax.broadcasted_iota(jnp.int32, (rows, width), 1)
    offset = col % tile_size
    source = col
    for step in range(1 - tile_size, tile_size):
        near = dest if step == 0 else pltpu.roll(dest, (-step) % width, 1)
        inside = (offset + step >= 0) & (offset + step < tile_size)
        source = jnp.where((near == offset) & inside, col + step, source)
    return source


def fused(
    count,
    bands,
    scaling,
    feat_ref,
    rad_ref,
    order_ref,
    first_ref,
    second_ref,
    third_ref,
    conv_one_ref,
    conv_two_ref,
    kern_one_ref,
    kern_two_ref,
    out_ref,
    plane,
    light,
    emb,
    emb_bf,
    part,
    part_in,
    pooled,
    taps,
    logit,
    canvas,
    block,
    block_in,
    rim,
    rim_in,
    rs_send,
    rs_recv,
    ag_send,
    ag_recv,
    halo_send,
    halo_recv,
    cs_send,
    cs_recv,
    rim_send,
    rim_recv,
):
    channels, _, rows, width = feat_ref.shape
    tile_size = order_ref.shape[-1]
    emb_width = third_ref.shape[0]
    radius = KSIZE // 2
    share = rows // count
    tall = rows + 2 * radius
    cols = width // count
    lanes = block.shape[-1]
    fold = lanes // cols
    groups = 4 // fold
    me = lax.axis_index("samp")
    here = lax.axis_index("band")
    peers = [lax.rem(me + step, count) for step in range(1, count)]
    has_above = here > 0
    has_below = here < bands - 1

    barrier = pltpu.get_barrier_semaphore()
    for peer in peers:
        pl.semaphore_signal(barrier, inc=1, device_id={"samp": peer}, device_id_type=MESH)

    @pl.when(has_above)
    def _():
        pl.semaphore_signal(barrier, inc=1, device_id={"band": here - 1}, device_id_type=MESH)

    @pl.when(has_below)
    def _():
        pl.semaphore_signal(barrier, inc=1, device_id={"band": here + 1}, device_id_type=MESH)

    source = slots_to_sources(order_ref[0], tile_size, width)
    halves = []
    for start in range(0, width, lanes):
        halves.append((start, source[:, start : start + lanes] - start))

    def reorder(values):
        return [
            jnp.take_along_axis(
                values[:, start : start + lanes], index, axis=1, mode="promise_in_bounds"
            )
            for start, index in halves
        ]

    def strided(ref, start, size, stride):
        return jnp.concatenate(
            [ref[half, pl.ds(start, size, stride=stride), :] for half in range(ref.shape[0])],
            axis=1,
        )

    for chan in range(channels):
        for half, part_x in enumerate(reorder(feat_ref[chan, 0].astype(jnp.float32))):
            plane[half, chan * rows : (chan + 1) * rows, :] = part_x
    for chan in range(3):
        light[chan] = jnp.concatenate(reorder(rad_ref[chan, 0]), axis=1)

    for row in range(rows):
        x = strided(plane, row, channels, rows).astype(jnp.bfloat16)
        x = jnp.dot(first_ref[...], x, preferred_element_type=jnp.float32)
        x = jnp.maximum(x, 0.0).astype(jnp.bfloat16)
        x = jnp.dot(second_ref[...], x, preferred_element_type=jnp.float32)
        x = jnp.maximum(x, 0.0).astype(jnp.bfloat16)
        x = jnp.dot(third_ref[...], x, preferred_element_type=jnp.float32)
        emb[row] = x
        emb_bf[row] = x.astype(jnp.bfloat16)
        part[row] = x.astype(part.dtype)

    beside = jnp.minimum(here, 1) + jnp.minimum(bands - 1 - here, 1)
    pl.semaphore_wait(barrier, count - 1 + beside)

    sums = []
    for slot, peer in enumerate(peers):
        copy = pltpu.make_async_remote_copy(
            src_ref=part.at[pl.ds(peer * share, share)],
            dst_ref=part_in.at[slot],
            send_sem=rs_send.at[slot],
            recv_sem=rs_recv.at[slot],
            device_id={"samp": peer},
            device_id_type=MESH,
        )
        copy.start()
        sums.append(copy)
    total = emb[pl.ds(me * share, share)]
    for slot, copy in enumerate(sums):
        copy.wait_recv()
        total = total + part_in[slot].astype(jnp.float32)
    own = pl.ds(radius + me * share, share)
    pooled[own] = (total * scaling).astype(jnp.bfloat16)
    gathers = []
    for slot, peer in enumerate(peers):
        copy = pltpu.make_async_remote_copy(
            src_ref=pooled.at[own],
            dst_ref=pooled.at[own],
            send_sem=ag_send.at[slot],
            recv_sem=ag_recv.at[slot],
            device_id={"samp": peer},
            device_id_type=MESH,
        )
        copy.start()
        gathers.append(copy)
    for chan in range(4):
        canvas[chan] = jnp.zeros(canvas.shape[1:], jnp.float32)
    for copy in sums:
        copy.wait_send()
    for copy in gathers:
        copy.wait_recv()

    def halo(down):
        start = rows if down else radius
        goal = 0 if down else rows + radius
        return pltpu.make_async_remote_copy(
            src_ref=pooled.at[pl.ds(start, radius)],
            dst_ref=pooled.at[pl.ds(goal, radius)],
            send_sem=halo_send.at[int(down)],
            recv_sem=halo_recv.at[int(down)],
            device_id={"band": here + 1 if down else here - 1},
            device_id_type=MESH,
        )

    @pl.when(has_below)
    def _():
        halo(True).start()

    @pl.when(has_above)
    def _():
        halo(False).start()

    @pl.when(here == 0)
    def _():
        pooled[0:radius] = jnp.zeros((radius, emb_width, width), jnp.bfloat16)

    @pl.when(here == bands - 1)
    def _():
        pooled[rows + radius : tall] = jnp.zeros((radius, emb_width, width), jnp.bfloat16)

    depth = KSIZE * emb_width
    col = lax.broadcasted_iota(jnp.int32, (emb_width, width), 1)

    def spread_row(row):
        values = pooled[row].astype(jnp.float32)
        for col_off in range(KSIZE):
            shift = col_off - radius
            if shift == 0:
                moved = values
            else:
                moved = pltpu.roll(values, (-shift) % width, 1)
                moved = jnp.where((col + shift >= 0) & (col + shift < width), moved, 0.0)
            start = row * depth + col_off * emb_width
            taps[start : start + emb_width, :] = moved.astype(jnp.bfloat16)

    def weigh_row(row):
        stacked = taps[row * depth : row * depth + KSIZE * depth, :]
        hidden = jnp.dot(conv_one_ref[...], stacked, preferred_element_type=jnp.float32)
        hidden = jnp.maximum(hidden, 0.0).astype(jnp.bfloat16)
        context = jnp.dot(conv_two_ref[...], hidden, preferred_element_type=jnp.float32)
        both = jnp.concatenate([emb_bf[row], context.astype(jnp.bfloat16)], axis=0)
        hidden = jnp.dot(kern_one_ref[...], both, preferred_element_type=jnp.float32)
        hidden = jnp.maximum(hidden, 0.0).astype(jnp.bfloat16)
        start = row * (logit.shape[1] // rows)
        values = jnp.dot(kern_two_ref[...], hidden, preferred_element_type=jnp.float32)
        for half in range(logit.shape[0]):
            logit[half, start : start + KSIZE * KSIZE, :] = values[
                :, half * lanes : (half + 1) * lanes
            ]

    for row in range(radius, rows + radius):
        spread_row(row)
    inner = range(radius, rows - radius)
    for row in inner:
        weigh_row(row)

    @pl.when(has_above)
    def _():
        halo(True).wait_recv()

    @pl.when(has_below)
    def _():
        halo(False).wait_recv()

    for row in range(tall):
        if row < radius or row >= rows + radius:
            spread_row(row)
    for row in range(rows):
        if row not in inner:
            weigh_row(row)

    col = lax.broadcasted_iota(jnp.int32, (rows, width), 1)
    colours = [light[chan] for chan in range(3)]
    stride = logit.shape[1] // rows
    for row_off in range(KSIZE):
        sums_c = [None] * 4
        for col_off in range(KSIZE):
            shift = col_off - radius
            weight = jnp.exp(strided(logit, row_off * KSIZE + col_off, rows, stride))
            if shift != 0:
                weight = jnp.where((col + shift >= 0) & (col + shift < width), weight, 0.0)
            for chan in range(4):
                term = weight * colours[chan] if chan < 3 else weight
                if shift != 0:
                    term = pltpu.roll(term, shift % width, 1)
                sums_c[chan] = term if sums_c[chan] is None else sums_c[chan] + term
        for chan in range(4):
            canvas[chan, row_off : row_off + rows, :] += sums_c[chan]

    lane = lax.broadcasted_iota(jnp.int32, (tall, lanes), 1) // cols
    for owner in range(count):
        base = owner * cols // lanes * lanes
        at = owner * cols - base
        for group in range(groups):
            packed = None
            for place in range(fold):
                piece = canvas[group * fold + place, 0:tall, base : base + lanes]
                turn = (place * cols - at) % lanes
                if turn:
                    piece = pltpu.roll(piece, turn, 1)
                packed = piece if packed is None else jnp.where(lane == place, piece, packed)
            block[owner, group * tall : (group + 1) * tall, :] = packed
    splats = []
    for slot, peer in enumerate(peers):
        copy = pltpu.make_async_remote_copy(
            src_ref=block.at[peer],
            dst_ref=block_in.at[slot],
            send_sem=cs_send.at[slot],
            recv_sem=cs_recv.at[slot],
            device_id={"samp": peer},
            device_id_type=MESH,
        )
        copy.start()
        splats.append(copy)
    for copy in gathers:
        copy.wait_send()

    @pl.when(has_below)
    def _():
        halo(True).wait_send()

    @pl.when(has_above)
    def _():
        halo(False).wait_send()

    total = block[me]
    for slot, copy in enumerate(splats):
        copy.wait_recv()
        total = total + block_in[slot]
    for copy in splats:
        copy.wait_send()

    for group in range(groups):
        rim[0, group * radius : (group + 1) * radius, :] = total[
            group * tall : group * tall + radius
        ]
        rim[1, group * radius : (group + 1) * radius, :] = total[
            group * tall + tall - radius : (group + 1) * tall
        ]

    def edge(down):
        return pltpu.make_async_remote_copy(
            src_ref=rim.at[int(down)],
            dst_ref=rim_in.at[int(down)],
            send_sem=rim_send.at[int(down)],
            recv_sem=rim_recv.at[int(down)],
            device_id={"band": here + 1 if down else here - 1},
            device_id_type=MESH,
        )

    @pl.when(has_below)
    def _():
        edge(True).start()

    @pl.when(has_above)
    def _():
        edge(False).start()

    @pl.when(here == 0)
    def _():
        rim_in[1] = jnp.zeros(rim_in.shape[1:], jnp.float32)

    @pl.when(here == bands - 1)
    def _():
        rim_in[0] = jnp.zeros(rim_in.shape[1:], jnp.float32)

    @pl.when(has_above)
    def _():
        edge(True).wait_recv()

    @pl.when(has_below)
    def _():
        edge(False).wait_recv()

    planes = []
    for group in range(groups):
        body = total[group * tall + radius : group * tall + radius + rows]
        above = rim_in[1, group * radius : (group + 1) * radius, :]
        below = rim_in[0, group * radius : (group + 1) * radius, :]
        gap = jnp.zeros((rows - 2 * radius, lanes), jnp.float32)
        body = body + jnp.concatenate([above, gap, below], axis=0)
        for place in range(fold):
            planes.append(pltpu.roll(body, lanes - place * cols, 1) if place else body)
    for chan in range(3):
        out_ref[chan] = (planes[chan] / planes[3])[:, :cols]

    @pl.when(has_below)
    def _():
        edge(True).wait_send()

    @pl.when(has_above)
    def _():
        edge(False).wait_send()


def fits(features, third, count):
    _, samples_dev, rows, width = features.shape
    radius = KSIZE // 2
    lanes = LANES
    cols = width // count
    return (
        samples_dev == 1
        and count > 1
        and rows % count == 0
        and rows % 8 == 0
        and rows >= 2 * radius
        and width % lanes == 0
        and lanes % cols == 0
        and lanes // cols in (1, 2, 4)
        and third.shape[0] % 16 == 0
    )


def fused_shards(
    features,
    radiance,
    sample_order,
    embed_first,
    embed_second,
    embed_third,
    conv_first,
    conv_second,
    kernel_first,
    kernel_second,
):
    count = lax.axis_size("samp")
    bands = lax.axis_size("band")
    channels, samples_dev, rows, width = features.shape
    emb_width = embed_third.shape[0]
    radius = KSIZE // 2
    tall = rows + 2 * radius
    cols = width // count
    groups = 4 * cols // LANES
    taps_pad = -(-KSIZE * KSIZE // 8) * 8
    scaling = 1.0 / math.sqrt(samples_dev * count)
    vmem = pl.BlockSpec(memory_space=pltpu.VMEM)
    sem = pltpu.SemaphoreType.DMA
    rim_rows = -(-groups * radius // 8) * 8
    return pl.pallas_call(
        functools.partial(fused, count, bands, scaling),
        out_shape=jax.ShapeDtypeStruct((3, rows, cols), jnp.float32),
        in_specs=[vmem] * 10,
        out_specs=vmem,
        scratch_shapes=[
            pltpu.VMEM((width // LANES, channels * rows, LANES), jnp.float32),
            pltpu.VMEM((3, rows, width), jnp.float32),
            pltpu.VMEM((rows, emb_width, width), jnp.float32),
            pltpu.VMEM((rows, emb_width, width), jnp.bfloat16),
            pltpu.VMEM((rows, emb_width, width), SENT),
            pltpu.VMEM((count - 1, rows // count, emb_width, width), SENT),
            pltpu.VMEM((tall, emb_width, width), jnp.bfloat16),
            pltpu.VMEM((tall * KSIZE * emb_width, width), jnp.bfloat16),
            pltpu.VMEM((width // LANES, rows * taps_pad, LANES), jnp.float32),
            pltpu.VMEM((4, -(-tall // 8) * 8, width), jnp.float32),
            pltpu.VMEM((count, groups * tall, LANES), jnp.float32),
            pltpu.VMEM((count - 1, groups * tall, LANES), jnp.float32),
            pltpu.VMEM((2, rim_rows, LANES), jnp.float32),
            pltpu.VMEM((2, rim_rows, LANES), jnp.float32),
            sem((count - 1,)),
            sem((count - 1,)),
            sem((count - 1,)),
            sem((count - 1,)),
            sem((2,)),
            sem((2,)),
            sem((count - 1,)),
            sem((count - 1,)),
            sem((2,)),
            sem((2,)),
        ],
        compiler_params=pltpu.CompilerParams(collective_id=0, has_side_effects=True),
    )(
        features,
        radiance,
        sample_order,
        embed_first,
        embed_second,
        embed_third,
        conv_first,
        conv_second,
        kernel_first,
        kernel_second,
    )


def either(*operands):
    if fits(operands[0], operands[5], lax.axis_size("samp")):
        return fused_shards(*operands)
    return shards(*operands)


def solution(mesh):
    in_specs = (
        P(None, ("group", "samp"), "band", None),
        P(None, ("group", "samp"), "band", None),
        P(("group", "samp"), "band", None, None),
        P(),
        P(),
        P(),
        P(),
        P(),
        P(),
        P(),
    )
    out_specs = P(None, ("group", "band"), "samp")
    return jax.shard_map(either, mesh=mesh, in_specs=in_specs, out_specs=out_specs, check_vma=False)
```

```python
import functools
import math

import jax
import jax.numpy as jnp
from jax import lax
from jax.experimental import pallas as pl
from jax.experimental.pallas import tpu as pltpu
from jax.sharding import PartitionSpec as P

KSIZE = 5
LANES = 128
SENT = jnp.float32


def padded_2(cells, sides, width):
    for axis, dim in sides:
        count = lax.axis_size(axis)
        ends = count - 1
        head = lax.slice_in_dim(cells, 0, width, axis=dim)
        tail = lax.slice_in_dim(cells, cells.shape[dim] - width, cells.shape[dim], axis=dim)
        cells = jnp.concatenate(
            [
                lax.ppermute(tail, axis, [(i, (i + 1) % count) for i in range(ends)]),
                cells,
                lax.ppermute(head, axis, [((i + 1) % count, i) for i in range(ends)]),
            ],
            axis=dim,
        )
    return cells


def passed_along(block, axis, distance):
    devices = range(lax.axis_size(axis))
    route = [(i - distance, i) for i in devices if i - distance in devices]
    return lax.ppermute(block, axis, route)


def to_pixels(values, sample_order):
    tile_size = sample_order.shape[-1]
    dest_cols = sample_order.reshape(sample_order.shape[:-2] + (-1,))
    offsets = jnp.arange(dest_cols.shape[-1], dtype=jnp.int32) % tile_size
    result = jnp.zeros_like(values)
    for slot_id in range(tile_size):
        spread = jnp.repeat(values[..., slot_id::tile_size], tile_size, axis=-1)
        target = jnp.repeat(dest_cols[..., slot_id::tile_size], tile_size, axis=-1)
        result = jnp.where((target == offsets)[None], spread, result)
    return result


def embed_samples(columns, embed_first, embed_second, embed_third):
    layer_one = jax.nn.relu(
        jnp.dot(embed_first, columns, preferred_element_type=jnp.float32)
    ).astype(jnp.bfloat16)
    layer_two = jax.nn.relu(
        jnp.dot(embed_second, layer_one, preferred_element_type=jnp.float32)
    ).astype(jnp.bfloat16)
    return jnp.dot(embed_third, layer_two, preferred_element_type=jnp.float32)


def convolve(padded, row_count, col_count, conv_first, conv_second):
    shifted = [
        padded[:, row_off : row_off + row_count, col_off : col_off + col_count]
        for row_off in range(KSIZE)
        for col_off in range(KSIZE)
    ]
    stacked = jnp.stack(shifted).reshape(-1, row_count * col_count)
    hidden = jax.nn.relu(jnp.dot(conv_first, stacked, preferred_element_type=jnp.float32)).astype(
        jnp.bfloat16
    )
    result = jnp.dot(conv_second, hidden, preferred_element_type=jnp.float32).astype(jnp.bfloat16)
    return result.reshape(-1, row_count, col_count)


def shards(
    features,
    radiance,
    sample_order,
    embed_first,
    embed_second,
    embed_third,
    conv_first,
    conv_second,
    kernel_first,
    kernel_second,
):
    ordered = to_pixels(features, sample_order)
    lights = to_pixels(radiance, sample_order)
    channels, samples_dev, row_count, crop_width = ordered.shape
    emb_width = embed_third.shape[0]
    radius = KSIZE // 2
    scaling = 1.0 / math.sqrt(samples_dev * lax.axis_size("samp"))
    embedded = embed_samples(ordered.reshape(channels, -1), embed_first, embed_second, embed_third)
    emb_bf = embedded.astype(jnp.bfloat16)
    own_part = jnp.dot(kernel_first[:, :emb_width], emb_bf, preferred_element_type=jnp.float32)
    own_part = own_part.reshape(-1, samples_dev, row_count, crop_width)
    partial_value = jnp.sum(embedded.reshape(emb_width, samples_dev, row_count, crop_width), axis=1)
    summed_emb = lax.psum(partial_value, "samp")
    pooled = (summed_emb * scaling).astype(jnp.bfloat16)
    padded = padded_2(pooled, (("band", 1),), 2)
    padded = jnp.pad(padded, ((0, 0), (0, 0), (radius, radius)))
    context = convolve(padded, row_count, crop_width, conv_first, conv_second)
    col_count = context.shape[2]
    ctx_part = jnp.dot(
        kernel_first[:, emb_width:],
        context.reshape(emb_width, -1),
        preferred_element_type=jnp.float32,
    )
    ctx_part = ctx_part.reshape(-1, 1, row_count, col_count)
    hidden = jax.nn.relu(own_part + ctx_part).astype(jnp.bfloat16)
    logits = jnp.dot(
        kernel_second, hidden.reshape(hidden.shape[0], -1), preferred_element_type=jnp.float32
    )
    weights = jnp.exp(logits).reshape(-1, samples_dev, row_count, col_count)
    with_ones = jnp.concatenate(
        [lights, jnp.ones((1, samples_dev, row_count, crop_width), jnp.float32)], axis=0
    )
    canvas = jnp.zeros((4, row_count + 2 * radius, crop_width + 2 * radius), jnp.float32)
    for row_off in range(KSIZE):
        for col_off in range(KSIZE):
            tap_index = row_off * KSIZE + col_off
            contrib = jnp.sum(weights[tap_index][None] * with_ones, axis=1)
            canvas = canvas.at[
                :, row_off : row_off + row_count, col_off : col_off + crop_width
            ].add(contrib)
    canvas = canvas[:, :, radius : radius + crop_width]
    summed_all = lax.psum_scatter(canvas, "samp", scatter_dimension=2, tiled=True)
    top_rims = summed_all[:, :radius]
    low_rims = summed_all[:, radius + row_count :]
    summed = summed_all[:, radius : radius + row_count]
    from_below = passed_along(top_rims, "band", -1)
    from_above = passed_along(low_rims, "band", 1)
    summed = summed.at[:, row_count - radius :].add(from_below)
    summed = summed.at[:, :radius].add(from_above)
    return summed[:3] / summed[3:4]


MESH = pl.DeviceIdType.MESH


def slots_to_sources(order, width):
    rows, tile_size, tiles = order.shape
    flat = order.reshape(rows * tile_size, tiles).astype(jnp.float32).astype(jnp.bfloat16)
    tile = lax.broadcasted_iota(jnp.int32, (tiles, width), 0)
    col = lax.broadcasted_iota(jnp.int32, (tiles, width), 1)
    spread = jnp.where(tile == col // tile_size, 1.0, 0.0).astype(jnp.bfloat16)
    wide = jnp.dot(flat, spread, preferred_element_type=jnp.float32).astype(jnp.int32)
    slot = lax.broadcasted_iota(jnp.int32, (rows * tile_size, width), 0) % tile_size
    offset = lax.broadcasted_iota(jnp.int32, (rows * tile_size, width), 1) % tile_size
    wide = jnp.where(wide == offset, slot, 0)
    slots = jnp.sum(wide.reshape(rows, tile_size, width), axis=1)
    col = lax.broadcasted_iota(jnp.int32, (rows, width), 1)
    return col // tile_size * tile_size + slots


def share_of(device, count):
    if count % 2:
        return device
    return device + 1 - 2 * (device % 2)


def fused(
    count,
    bands,
    scaling,
    feat_ref,
    rad_ref,
    order_ref,
    first_turned,
    second_ref,
    third_ref,
    conv_one_turned,
    conv_two_ref,
    kern_one_turned,
    kern_two_ref,
    out_ref,
    first_ref,
    conv_one_ref,
    kern_one_ref,
    plane,
    light,
    emb_bf,
    part,
    part_in,
    pooled,
    taps,
    logit,
    canvas,
    block,
    block_in,
    rim,
    rim_in,
    rs_send,
    rs_recv,
    ag_send,
    ag_recv,
    halo_send,
    halo_recv,
    cs_send,
    cs_recv,
    rim_send,
    rim_recv,
):
    channels, _, rows, width = feat_ref.shape
    emb_width = third_ref.shape[0]
    radius = KSIZE // 2
    share = rows // count
    tall = rows + 2 * radius
    cols = width // count
    lanes = block.shape[-1]
    fold = lanes // cols
    groups = 4 // fold
    me = lax.axis_index("samp")
    here = lax.axis_index("band")
    peers = [lax.rem(me + step, count) for step in range(1, count)]
    chunk = share_of(me, count)
    has_above = here > 0
    has_below = here < bands - 1

    barrier = pltpu.get_barrier_semaphore()
    for peer in peers:
        pl.semaphore_signal(barrier, inc=1, device_id={"samp": peer}, device_id_type=MESH)

    @pl.when(has_above)
    def _():
        for peer in [me] + peers:
            pl.semaphore_signal(
                barrier,
                inc=1,
                device_id={"samp": peer, "band": here - 1},
                device_id_type=MESH,
            )

    @pl.when(has_below)
    def _():
        for peer in [me] + peers:
            pl.semaphore_signal(
                barrier,
                inc=1,
                device_id={"samp": peer, "band": here + 1},
                device_id_type=MESH,
            )

    source = slots_to_sources(order_ref[0], width)
    halves = []
    for start in range(0, width, lanes):
        halves.append((start, source[:, start : start + lanes] - start))

    def reorder(values):
        return [
            jnp.take_along_axis(
                values[:, start : start + lanes], index, axis=1, mode="promise_in_bounds"
            )
            for start, index in halves
        ]

    def strided(ref, start, size, stride):
        return jnp.concatenate(
            [ref[half, pl.ds(start, size, stride=stride), :] for half in range(ref.shape[0])],
            axis=1,
        )

    for chan in range(channels):
        for half, part_x in enumerate(reorder(feat_ref[chan, 0].astype(jnp.float32))):
            plane[half, chan * rows : (chan + 1) * rows, :] = part_x
    for chan in range(3):
        light[chan] = jnp.concatenate(reorder(rad_ref[chan, 0]), axis=1)

    first_ref[...] = first_turned[...].T

    def embed_row(row):
        x = strided(plane, row, channels, rows).astype(jnp.bfloat16)
        x = jnp.dot(first_ref[...], x, preferred_element_type=jnp.float32)
        x = jnp.maximum(x, 0.0).astype(jnp.bfloat16)
        x = jnp.dot(second_ref[...], x, preferred_element_type=jnp.float32)
        x = jnp.maximum(x, 0.0).astype(jnp.bfloat16)
        x = jnp.dot(third_ref[...], x, preferred_element_type=jnp.float32)
        emb_bf[row] = x.astype(jnp.bfloat16)
        return x

    beside = jnp.minimum(here, 1) + jnp.minimum(bands - 1 - here, 1)
    sums = []
    for slot, peer in enumerate(peers):
        start = share_of(peer, count) * share
        for row in range(share):
            part[slot, row] = embed_row(start + row).astype(part.dtype)
        if slot == 0:
            pl.semaphore_wait(barrier, count - 1 + beside * count)
        copy = pltpu.make_async_remote_copy(
            src_ref=part.at[slot],
            dst_ref=part_in.at[slot],
            send_sem=rs_send.at[slot],
            recv_sem=rs_recv.at[slot],
            device_id={"samp": peer},
            device_id_type=MESH,
        )
        copy.start()
        sums.append(copy)
    total = [embed_row(chunk * share + row) for row in range(share)]
    conv_one_ref[...] = conv_one_turned[...].T
    kern_one_ref[...] = kern_one_turned[...].T
    canvas[...] = jnp.zeros(canvas.shape, jnp.float32)
    for slot, copy in enumerate(sums):
        copy.wait_recv()
        for row in range(share):
            total[row] = total[row] + part_in[slot, row].astype(jnp.float32)
    for row in range(share):
        pooled[radius + chunk * share + row] = (total[row] * scaling).astype(jnp.bfloat16)

    def gather(slot, peer, sender):
        rows_of = pl.ds(radius + share_of(sender, count) * share, share)
        return pltpu.make_async_remote_copy(
            src_ref=pooled.at[rows_of],
            dst_ref=pooled.at[rows_of],
            send_sem=ag_send.at[slot],
            recv_sem=ag_recv.at[sender],
            device_id={"samp": peer},
            device_id_type=MESH,
        )

    gathers = [gather(slot, peer, me) for slot, peer in enumerate(peers)]
    for copy in gathers:
        copy.start()

    def halo(down):
        start = rows if down else radius
        goal = 0 if down else rows + radius
        return pltpu.make_async_remote_copy(
            src_ref=pooled.at[pl.ds(start, radius)],
            dst_ref=pooled.at[pl.ds(goal, radius)],
            send_sem=halo_send.at[int(down)],
            recv_sem=halo_recv.at[int(down)],
            device_id={"band": here + 1 if down else here - 1},
            device_id_type=MESH,
        )

    @pl.when(here == 0)
    def _():
        pooled[0:radius] = jnp.zeros((radius, emb_width, width), jnp.bfloat16)

    @pl.when(here == bands - 1)
    def _():
        pooled[rows + radius : tall] = jnp.zeros((radius, emb_width, width), jnp.bfloat16)

    depth = KSIZE * emb_width
    col = lax.broadcasted_iota(jnp.int32, (emb_width, width), 1)

    def spread_row(row):
        values = pooled[row].astype(jnp.float32)
        for col_off in range(KSIZE):
            shift = col_off - radius
            if shift == 0:
                moved = values
            else:
                moved = pltpu.roll(values, (-shift) % width, 1)
                moved = jnp.where((col + shift >= 0) & (col + shift < width), moved, 0.0)
            start = row * depth + col_off * emb_width
            taps[start : start + emb_width, :] = moved.astype(jnp.bfloat16)

    def weigh_row(row):
        stacked = taps[row * depth : row * depth + KSIZE * depth, :]
        hidden = jnp.dot(conv_one_ref[...], stacked, preferred_element_type=jnp.float32)
        hidden = jnp.maximum(hidden, 0.0).astype(jnp.bfloat16)
        context = jnp.dot(conv_two_ref[...], hidden, preferred_element_type=jnp.float32)
        both = jnp.concatenate([emb_bf[row], context.astype(jnp.bfloat16)], axis=0)
        hidden = jnp.dot(kern_one_ref[...], both, preferred_element_type=jnp.float32)
        hidden = jnp.maximum(hidden, 0.0).astype(jnp.bfloat16)
        start = row * (logit.shape[1] // rows)
        values = jnp.dot(kern_two_ref[...], hidden, preferred_element_type=jnp.float32)
        for half in range(logit.shape[0]):
            logit[half, start : start + KSIZE * KSIZE, :] = values[
                :, half * lanes : (half + 1) * lanes
            ]

    edges = -(-radius // share)
    order = list(range(edges)) + list(range(count - edges, count))
    order = list(dict.fromkeys(order))
    order += [share_id for share_id in range(count) if share_id not in order]
    for place, share_id in enumerate(order):
        owner = share_of(share_id, count)

        @pl.when(me != owner)
        def _():
            gather(0, peers[0], owner).wait_recv()

        if place == edges - 1:

            @pl.when(has_above)
            def _():
                halo(False).start()

        if place == min(2 * edges, count) - 1:

            @pl.when(has_below)
            def _():
                halo(True).start()

        if place >= min(2 * edges, count) - 1:
            ready = order[: place + 1] if place == min(2 * edges, count) - 1 else [share_id]
            for done in ready:
                for row in range(share):
                    spread_row(radius + done * share + row)
    inner = range(radius, rows - radius)
    for row in inner:
        weigh_row(row)

    @pl.when(has_above)
    def _():
        halo(True).wait_recv()

    @pl.when(has_below)
    def _():
        halo(False).wait_recv()

    for row in range(tall):
        if row < radius or row >= rows + radius:
            spread_row(row)
    for row in range(rows):
        if row not in inner:
            weigh_row(row)

    col = lax.broadcasted_iota(jnp.int32, (rows, width), 1)
    colours = [light[chan] for chan in range(3)]
    stride = logit.shape[1] // rows
    for row_off in range(KSIZE):
        sums_c = [None] * 4
        for col_off in range(KSIZE):
            shift = col_off - radius
            weight = jnp.exp(strided(logit, row_off * KSIZE + col_off, rows, stride))
            if shift != 0:
                weight = jnp.where((col + shift >= 0) & (col + shift < width), weight, 0.0)
            for chan in range(4):
                term = weight * colours[chan] if chan < 3 else weight
                if shift != 0:
                    term = pltpu.roll(term, shift % width, 1)
                sums_c[chan] = term if sums_c[chan] is None else sums_c[chan] + term
        for chan in range(4):
            canvas[chan, row_off : row_off + rows, :] += sums_c[chan]

    lane = lax.broadcasted_iota(jnp.int32, (tall, lanes), 1) // cols
    for owner in range(count):
        base = owner * cols // lanes * lanes
        at = owner * cols - base
        for group in range(groups):
            packed = None
            for place in range(fold):
                piece = canvas[group * fold + place, 0:tall, base : base + lanes]
                turn = (place * cols - at) % lanes
                if turn:
                    piece = pltpu.roll(piece, turn, 1)
                packed = piece if packed is None else jnp.where(lane == place, piece, packed)
            block[owner, group * rows : (group + 1) * rows, :] = packed[radius : radius + rows]
            at_rim = pl.ds(group * radius, radius)
            rim[0, owner, at_rim, :] = packed[:radius]
            rim[1, owner, at_rim, :] = packed[tall - radius :]

    def edge(down, slot, peer):
        return pltpu.make_async_remote_copy(
            src_ref=rim.at[int(down), peer],
            dst_ref=rim_in.at[int(down), slot],
            send_sem=rim_send.at[int(down), slot],
            recv_sem=rim_recv.at[int(down), slot],
            device_id={"samp": peer, "band": here + 1 if down else here - 1},
            device_id_type=MESH,
        )

    @pl.when(has_below)
    def _():
        for slot, peer in enumerate([me] + peers):
            edge(True, slot, peer).start()

    @pl.when(has_above)
    def _():
        for slot, peer in enumerate([me] + peers):
            edge(False, slot, peer).start()

    splats = []
    for slot, peer in enumerate(peers):
        copy = pltpu.make_async_remote_copy(
            src_ref=block.at[peer],
            dst_ref=block_in.at[slot],
            send_sem=cs_send.at[slot],
            recv_sem=cs_recv.at[slot],
            device_id={"samp": peer},
            device_id_type=MESH,
        )
        copy.start()
        splats.append(copy)
    for copy in sums + gathers:
        copy.wait_send()

    @pl.when(has_below)
    def _():
        halo(True).wait_send()

    @pl.when(has_above)
    def _():
        halo(False).wait_send()

    @pl.when(here == 0)
    def _():
        rim_in[1] = jnp.zeros(rim_in.shape[1:], jnp.float32)

    @pl.when(here == bands - 1)
    def _():
        rim_in[0] = jnp.zeros(rim_in.shape[1:], jnp.float32)

    total = block[me]
    for slot, copy in enumerate(splats):
        copy.wait_recv()
        total = total + block_in[slot]

    @pl.when(has_above)
    def _():
        for slot, peer in enumerate([me] + peers):
            edge(True, slot, peer).wait_recv()

    @pl.when(has_below)
    def _():
        for slot, peer in enumerate([me] + peers):
            edge(False, slot, peer).wait_recv()

    below = rim_in[0, 0]
    above = rim_in[1, 0]
    for slot in range(1, count):
        below = below + rim_in[0, slot]
        above = above + rim_in[1, slot]

    planes = []
    for group in range(groups):
        near = slice(group * radius, (group + 1) * radius)
        gap = jnp.zeros((rows - 2 * radius, lanes), jnp.float32)
        body = total[group * rows : (group + 1) * rows]
        body = body + jnp.concatenate([above[near], gap, below[near]], axis=0)
        for place in range(fold):
            planes.append(pltpu.roll(body, lanes - place * cols, 1) if place else body)
    for chan in range(3):
        out_ref[chan] = (planes[chan] / planes[3])[:, :cols]
    for copy in splats:
        copy.wait_send()

    @pl.when(has_below)
    def _():
        for slot, peer in enumerate([me] + peers):
            edge(True, slot, peer).wait_send()

    @pl.when(has_above)
    def _():
        for slot, peer in enumerate([me] + peers):
            edge(False, slot, peer).wait_send()


def fits(features, third, count):
    _, samples_dev, rows, width = features.shape
    radius = KSIZE // 2
    lanes = LANES
    cols = width // count
    return (
        samples_dev == 1
        and count > 1
        and rows % count == 0
        and rows % 8 == 0
        and rows >= 2 * radius
        and width % lanes == 0
        and lanes % cols == 0
        and lanes // cols in (1, 2, 4)
        and third.shape[0] % 16 == 0
    )


def fused_shards(
    features,
    radiance,
    sample_order,
    embed_first,
    embed_second,
    embed_third,
    conv_first,
    conv_second,
    kernel_first,
    kernel_second,
):
    count = lax.axis_size("samp")
    bands = lax.axis_size("band")
    channels, samples_dev, rows, width = features.shape
    emb_width = embed_third.shape[0]
    radius = KSIZE // 2
    tall = rows + 2 * radius
    cols = width // count
    groups = 4 * cols // LANES
    taps_pad = -(-KSIZE * KSIZE // 8) * 8
    scaling = 1.0 / math.sqrt(samples_dev * count)
    vmem = pl.BlockSpec(memory_space=pltpu.VMEM)
    sem = pltpu.SemaphoreType.DMA
    rim_rows = -(-groups * radius // 8) * 8
    return pl.pallas_call(
        functools.partial(fused, count, bands, scaling),
        out_shape=jax.ShapeDtypeStruct((3, rows, cols), jnp.float32),
        in_specs=[vmem] * 10,
        out_specs=vmem,
        scratch_shapes=[
            pltpu.VMEM(embed_first.shape, jnp.bfloat16),
            pltpu.VMEM(conv_first.shape, jnp.bfloat16),
            pltpu.VMEM(kernel_first.shape, jnp.bfloat16),
            pltpu.VMEM((width // LANES, channels * rows, LANES), jnp.float32),
            pltpu.VMEM((3, rows, width), jnp.float32),
            pltpu.VMEM((rows, emb_width, width), jnp.bfloat16),
            pltpu.VMEM((count - 1, rows // count, emb_width, width), SENT),
            pltpu.VMEM((count - 1, rows // count, emb_width, width), SENT),
            pltpu.VMEM((tall, emb_width, width), jnp.bfloat16),
            pltpu.VMEM((tall * KSIZE * emb_width, width), jnp.bfloat16),
            pltpu.VMEM((width // LANES, rows * taps_pad, LANES), jnp.float32),
            pltpu.VMEM((4, -(-tall // 8) * 8, width), jnp.float32),
            pltpu.VMEM((count, groups * rows, LANES), jnp.float32),
            pltpu.VMEM((count - 1, groups * rows, LANES), jnp.float32),
            pltpu.VMEM((2, count, rim_rows, LANES), jnp.float32),
            pltpu.VMEM((2, count, rim_rows, LANES), jnp.float32),
            sem((count - 1,)),
            sem((count - 1,)),
            sem((count - 1,)),
            sem((count,)),
            sem((2,)),
            sem((2,)),
            sem((count - 1,)),
            sem((count - 1,)),
            sem((2, count)),
            sem((2, count)),
        ],
        compiler_params=pltpu.CompilerParams(collective_id=0, has_side_effects=True),
    )(
        features,
        radiance,
        jnp.swapaxes(sample_order, 2, 3),
        embed_first.T,
        embed_second,
        embed_third,
        conv_first.T,
        conv_second,
        kernel_first.T,
        kernel_second,
    )


def either(*operands):
    if fits(operands[0], operands[5], lax.axis_size("samp")):
        return fused_shards(*operands)
    return shards(*operands)


def solution(mesh):
    in_specs = (
        P(None, ("group", "samp"), "band", None),
        P(None, ("group", "samp"), "band", None),
        P(("group", "samp"), "band", None, None),
        P(),
        P(),
        P(),
        P(),
        P(),
        P(),
        P(),
    )
    out_specs = P(None, ("group", "band"), "samp")
    return jax.shard_map(either, mesh=mesh, in_specs=in_specs, out_specs=out_specs, check_vma=False)
```

```python
import functools
import math

import jax
import jax.numpy as jnp
from jax import lax
from jax.experimental import pallas as pl
from jax.experimental.pallas import tpu as pltpu
from jax.sharding import PartitionSpec as P

KSIZE = 5
LANES = 128
SENT = jnp.float32


def padded_2(cells, sides, width):
    for axis, dim in sides:
        count = lax.axis_size(axis)
        ends = count - 1
        head = lax.slice_in_dim(cells, 0, width, axis=dim)
        tail = lax.slice_in_dim(cells, cells.shape[dim] - width, cells.shape[dim], axis=dim)
        cells = jnp.concatenate(
            [
                lax.ppermute(tail, axis, [(i, (i + 1) % count) for i in range(ends)]),
                cells,
                lax.ppermute(head, axis, [((i + 1) % count, i) for i in range(ends)]),
            ],
            axis=dim,
        )
    return cells


def passed_along(block, axis, distance):
    devices = range(lax.axis_size(axis))
    route = [(i - distance, i) for i in devices if i - distance in devices]
    return lax.ppermute(block, axis, route)


def to_pixels(values, sample_order):
    tile_size = sample_order.shape[-1]
    dest_cols = sample_order.reshape(sample_order.shape[:-2] + (-1,))
    offsets = jnp.arange(dest_cols.shape[-1], dtype=jnp.int32) % tile_size
    result = jnp.zeros_like(values)
    for slot_id in range(tile_size):
        spread = jnp.repeat(values[..., slot_id::tile_size], tile_size, axis=-1)
        target = jnp.repeat(dest_cols[..., slot_id::tile_size], tile_size, axis=-1)
        result = jnp.where((target == offsets)[None], spread, result)
    return result


def embed_samples(columns, embed_first, embed_second, embed_third):
    layer_one = jax.nn.relu(
        jnp.dot(embed_first, columns, preferred_element_type=jnp.float32)
    ).astype(jnp.bfloat16)
    layer_two = jax.nn.relu(
        jnp.dot(embed_second, layer_one, preferred_element_type=jnp.float32)
    ).astype(jnp.bfloat16)
    return jnp.dot(embed_third, layer_two, preferred_element_type=jnp.float32)


def convolve(padded, row_count, col_count, conv_first, conv_second):
    shifted = [
        padded[:, row_off : row_off + row_count, col_off : col_off + col_count]
        for row_off in range(KSIZE)
        for col_off in range(KSIZE)
    ]
    stacked = jnp.stack(shifted).reshape(-1, row_count * col_count)
    hidden = jax.nn.relu(jnp.dot(conv_first, stacked, preferred_element_type=jnp.float32)).astype(
        jnp.bfloat16
    )
    result = jnp.dot(conv_second, hidden, preferred_element_type=jnp.float32).astype(jnp.bfloat16)
    return result.reshape(-1, row_count, col_count)


def shards(
    features,
    radiance,
    sample_order,
    embed_first,
    embed_second,
    embed_third,
    conv_first,
    conv_second,
    kernel_first,
    kernel_second,
):
    ordered = to_pixels(features, sample_order)
    lights = to_pixels(radiance, sample_order)
    channels, samples_dev, row_count, crop_width = ordered.shape
    emb_width = embed_third.shape[0]
    radius = KSIZE // 2
    scaling = 1.0 / math.sqrt(samples_dev * lax.axis_size("samp"))
    embedded = embed_samples(ordered.reshape(channels, -1), embed_first, embed_second, embed_third)
    emb_bf = embedded.astype(jnp.bfloat16)
    own_part = jnp.dot(kernel_first[:, :emb_width], emb_bf, preferred_element_type=jnp.float32)
    own_part = own_part.reshape(-1, samples_dev, row_count, crop_width)
    partial_value = jnp.sum(embedded.reshape(emb_width, samples_dev, row_count, crop_width), axis=1)
    summed_emb = lax.psum(partial_value, "samp")
    pooled = (summed_emb * scaling).astype(jnp.bfloat16)
    padded = padded_2(pooled, (("band", 1),), 2)
    padded = jnp.pad(padded, ((0, 0), (0, 0), (radius, radius)))
    context = convolve(padded, row_count, crop_width, conv_first, conv_second)
    col_count = context.shape[2]
    ctx_part = jnp.dot(
        kernel_first[:, emb_width:],
        context.reshape(emb_width, -1),
        preferred_element_type=jnp.float32,
    )
    ctx_part = ctx_part.reshape(-1, 1, row_count, col_count)
    hidden = jax.nn.relu(own_part + ctx_part).astype(jnp.bfloat16)
    logits = jnp.dot(
        kernel_second, hidden.reshape(hidden.shape[0], -1), preferred_element_type=jnp.float32
    )
    weights = jnp.exp(logits).reshape(-1, samples_dev, row_count, col_count)
    with_ones = jnp.concatenate(
        [lights, jnp.ones((1, samples_dev, row_count, crop_width), jnp.float32)], axis=0
    )
    canvas = jnp.zeros((4, row_count + 2 * radius, crop_width + 2 * radius), jnp.float32)
    for row_off in range(KSIZE):
        for col_off in range(KSIZE):
            tap_index = row_off * KSIZE + col_off
            contrib = jnp.sum(weights[tap_index][None] * with_ones, axis=1)
            canvas = canvas.at[
                :, row_off : row_off + row_count, col_off : col_off + crop_width
            ].add(contrib)
    canvas = canvas[:, :, radius : radius + crop_width]
    summed_all = lax.psum_scatter(canvas, "samp", scatter_dimension=2, tiled=True)
    top_rims = summed_all[:, :radius]
    low_rims = summed_all[:, radius + row_count :]
    summed = summed_all[:, radius : radius + row_count]
    from_below = passed_along(top_rims, "band", -1)
    from_above = passed_along(low_rims, "band", 1)
    summed = summed.at[:, row_count - radius :].add(from_below)
    summed = summed.at[:, :radius].add(from_above)
    return summed[:3] / summed[3:4]


MESH = pl.DeviceIdType.MESH


def slots_to_sources(order, width):
    rows, tile_size, tiles = order.shape
    flat = order.reshape(rows * tile_size, tiles).astype(jnp.float32).astype(jnp.bfloat16)
    tile = lax.broadcasted_iota(jnp.int32, (tiles, width), 0)
    col = lax.broadcasted_iota(jnp.int32, (tiles, width), 1)
    spread = jnp.where(tile == col // tile_size, 1.0, 0.0).astype(jnp.bfloat16)
    wide = jnp.dot(flat, spread, preferred_element_type=jnp.float32).astype(jnp.int32)
    slot = lax.broadcasted_iota(jnp.int32, (rows * tile_size, width), 0) % tile_size
    offset = lax.broadcasted_iota(jnp.int32, (rows * tile_size, width), 1) % tile_size
    wide = jnp.where(wide == offset, slot, 0)
    slots = jnp.sum(wide.reshape(rows, tile_size, width), axis=1)
    col = lax.broadcasted_iota(jnp.int32, (rows, width), 1)
    return col // tile_size * tile_size + slots


def share_of(device, count):
    if count % 2:
        return device
    return device + 1 - 2 * (device % 2)


def staged(count, bands, scaling, *refs):
    sources, held, load_sem = refs[:10], refs[-11:-1], refs[-1]
    loads = [
        pltpu.make_async_copy(source, target, load_sem.at[place])
        for place, (source, target) in enumerate(zip(sources, held))
    ]
    fused(count, bands, scaling, loads, *held, *refs[10:-11])


def fused(
    count,
    bands,
    scaling,
    loads,
    feat_ref,
    rad_ref,
    order_ref,
    first_turned,
    second_ref,
    third_ref,
    conv_one_turned,
    conv_two_ref,
    kern_one_turned,
    kern_two_ref,
    out_ref,
    first_ref,
    conv_one_ref,
    kern_one_ref,
    plane,
    light,
    emb_bf,
    part,
    part_in,
    pooled,
    taps,
    logit,
    canvas,
    block,
    block_in,
    rim,
    rim_in,
    rs_send,
    rs_recv,
    ag_send,
    ag_recv,
    halo_send,
    halo_recv,
    cs_send,
    cs_recv,
    rim_send,
    rim_recv,
):
    channels, _, rows, width = feat_ref.shape
    emb_width = third_ref.shape[0]
    radius = KSIZE // 2
    share = rows // count
    tall = rows + 2 * radius
    cols = width // count
    lanes = block.shape[-1]
    fold = lanes // cols
    groups = 4 // fold
    me = lax.axis_index("samp")
    here = lax.axis_index("band")
    peers = [lax.rem(me + step, count) for step in range(1, count)]
    chunk = share_of(me, count)
    has_above = here > 0
    has_below = here < bands - 1

    barrier = pltpu.get_barrier_semaphore()
    for peer in peers:
        pl.semaphore_signal(barrier, inc=1, device_id={"samp": peer}, device_id_type=MESH)

    @pl.when(has_above)
    def _():
        pl.semaphore_signal(barrier, inc=1, device_id={"band": here - 1}, device_id_type=MESH)

    @pl.when(has_below)
    def _():
        pl.semaphore_signal(barrier, inc=1, device_id={"band": here + 1}, device_id_type=MESH)

    for place in (2, 0, 3, 4, 5, 1, 6, 8, 7, 9):
        loads[place].start()

    loads[2].wait()
    source = slots_to_sources(order_ref[0], width)
    halves = []
    for start in range(0, width, lanes):
        halves.append((start, source[:, start : start + lanes] - start))

    def reorder(values):
        return [
            jnp.take_along_axis(
                values[:, start : start + lanes], index, axis=1, mode="promise_in_bounds"
            )
            for start, index in halves
        ]

    def strided(ref, start, size, stride):
        return jnp.concatenate(
            [ref[half, pl.ds(start, size, stride=stride), :] for half in range(ref.shape[0])],
            axis=1,
        )

    loads[0].wait()
    for chan in range(channels):
        for half, part_x in enumerate(reorder(feat_ref[chan, 0].astype(jnp.float32))):
            plane[half, chan * rows : (chan + 1) * rows, :] = part_x
    loads[1].wait()
    for chan in range(3):
        light[chan] = jnp.concatenate(reorder(rad_ref[chan, 0]), axis=1)

    for place in (3, 4, 5):
        loads[place].wait()
    first_ref[...] = first_turned[...].T

    def embed_row(row):
        x = strided(plane, row, channels, rows).astype(jnp.bfloat16)
        x = jnp.dot(first_ref[...], x, preferred_element_type=jnp.float32)
        x = jnp.maximum(x, 0.0).astype(jnp.bfloat16)
        x = jnp.dot(second_ref[...], x, preferred_element_type=jnp.float32)
        x = jnp.maximum(x, 0.0).astype(jnp.bfloat16)
        x = jnp.dot(third_ref[...], x, preferred_element_type=jnp.float32)
        emb_bf[row] = x.astype(jnp.bfloat16)
        return x

    for slot, peer in enumerate(peers):
        start = share_of(peer, count) * share
        for row in range(share):
            part[slot, row] = embed_row(start + row).astype(part.dtype)
    total = [embed_row(chunk * share + row) for row in range(share)]
    for place in (6, 8, 7, 9):
        loads[place].wait()
    conv_one_ref[...] = conv_one_turned[...].T
    kern_one_ref[...] = kern_one_turned[...].T
    canvas[...] = jnp.zeros(canvas.shape, jnp.float32)

    beside = jnp.minimum(here, 1) + jnp.minimum(bands - 1 - here, 1)
    pl.semaphore_wait(barrier, count - 1 + beside)
    sums = []
    for row in range(share):
        for slot, peer in enumerate(peers):
            copy = pltpu.make_async_remote_copy(
                src_ref=part.at[slot, row],
                dst_ref=part_in.at[slot, row],
                send_sem=rs_send.at[slot, row],
                recv_sem=rs_recv.at[slot, row],
                device_id={"samp": peer},
                device_id_type=MESH,
            )
            copy.start()
            sums.append(copy)

    def gather(slot, row, peer, sender):
        at = radius + share_of(sender, count) * share + row
        return pltpu.make_async_remote_copy(
            src_ref=pooled.at[at],
            dst_ref=pooled.at[at],
            send_sem=ag_send.at[slot, row],
            recv_sem=ag_recv.at[sender, row],
            device_id={"samp": peer},
            device_id_type=MESH,
        )

    gathers = []
    for row in range(share):
        summed = total[row]
        for slot in range(count - 1):
            sums[row * (count - 1) + slot].wait_recv()
            summed = summed + part_in[slot, row].astype(jnp.float32)
        pooled[radius + chunk * share + row] = (summed * scaling).astype(jnp.bfloat16)
        for slot, peer in enumerate(peers):
            copy = gather(slot, row, peer, me)
            copy.start()
            gathers.append(copy)

    def halo(down):
        start = rows if down else radius
        goal = 0 if down else rows + radius
        return pltpu.make_async_remote_copy(
            src_ref=pooled.at[pl.ds(start, radius)],
            dst_ref=pooled.at[pl.ds(goal, radius)],
            send_sem=halo_send.at[int(down)],
            recv_sem=halo_recv.at[int(down)],
            device_id={"band": here + 1 if down else here - 1},
            device_id_type=MESH,
        )

    @pl.when(here == 0)
    def _():
        pooled[0:radius] = jnp.zeros((radius, emb_width, width), jnp.bfloat16)

    @pl.when(here == bands - 1)
    def _():
        pooled[rows + radius : tall] = jnp.zeros((radius, emb_width, width), jnp.bfloat16)

    depth = KSIZE * emb_width
    col = lax.broadcasted_iota(jnp.int32, (emb_width, width), 1)

    def spread_row(row):
        values = pooled[row].astype(jnp.float32)
        for col_off in range(KSIZE):
            shift = col_off - radius
            if shift == 0:
                moved = values
            else:
                moved = pltpu.roll(values, (-shift) % width, 1)
                moved = jnp.where((col + shift >= 0) & (col + shift < width), moved, 0.0)
            start = row * depth + col_off * emb_width
            taps[start : start + emb_width, :] = moved.astype(jnp.bfloat16)

    def weigh_row(row):
        stacked = taps[row * depth : row * depth + KSIZE * depth, :]
        hidden = jnp.dot(conv_one_ref[...], stacked, preferred_element_type=jnp.float32)
        hidden = jnp.maximum(hidden, 0.0).astype(jnp.bfloat16)
        context = jnp.dot(conv_two_ref[...], hidden, preferred_element_type=jnp.float32)
        both = jnp.concatenate([emb_bf[row], context.astype(jnp.bfloat16)], axis=0)
        hidden = jnp.dot(kern_one_ref[...], both, preferred_element_type=jnp.float32)
        hidden = jnp.maximum(hidden, 0.0).astype(jnp.bfloat16)
        start = row * (logit.shape[1] // rows)
        values = jnp.dot(kern_two_ref[...], hidden, preferred_element_type=jnp.float32)
        for half in range(logit.shape[0]):
            logit[half, start : start + KSIZE * KSIZE, :] = values[
                :, half * lanes : (half + 1) * lanes
            ]

    edges = -(-radius // share)
    order = list(range(edges)) + list(range(count - edges, count))
    order = list(dict.fromkeys(order))
    order += [share_id for share_id in range(count) if share_id not in order]
    for place, share_id in enumerate(order):
        owner = share_of(share_id, count)

        @pl.when(me != owner)
        def _():
            for row in range(share):
                gather(0, row, peers[0], owner).wait_recv()

        if place == edges - 1:

            @pl.when(has_above)
            def _():
                halo(False).start()

        if place == min(2 * edges, count) - 1:

            @pl.when(has_below)
            def _():
                halo(True).start()

        if place >= min(2 * edges, count) - 1:
            ready = order[: place + 1] if place == min(2 * edges, count) - 1 else [share_id]
            for done in ready:
                for row in range(share):
                    spread_row(radius + done * share + row)
    inner = range(radius, rows - radius)
    for row in inner:
        weigh_row(row)

    @pl.when(has_above)
    def _():
        halo(True).wait_recv()

    @pl.when(has_below)
    def _():
        halo(False).wait_recv()

    for row in range(tall):
        if row < radius or row >= rows + radius:
            spread_row(row)
    for row in range(rows):
        if row not in inner:
            weigh_row(row)

    col = lax.broadcasted_iota(jnp.int32, (rows, width), 1)
    colours = [light[chan] for chan in range(3)]
    stride = logit.shape[1] // rows
    for row_off in range(KSIZE):
        sums_c = [None] * 4
        for col_off in range(KSIZE):
            shift = col_off - radius
            weight = jnp.exp(strided(logit, row_off * KSIZE + col_off, rows, stride))
            if shift != 0:
                weight = jnp.where((col + shift >= 0) & (col + shift < width), weight, 0.0)
            for chan in range(4):
                term = weight * colours[chan] if chan < 3 else weight
                if shift != 0:
                    term = pltpu.roll(term, shift % width, 1)
                sums_c[chan] = term if sums_c[chan] is None else sums_c[chan] + term
        for chan in range(4):
            canvas[chan, row_off : row_off + rows, :] += sums_c[chan]

    lane = lax.broadcasted_iota(jnp.int32, (tall, lanes), 1) // cols
    for owner in range(count):
        base = owner * cols // lanes * lanes
        at = owner * cols - base
        for group in range(groups):
            packed = None
            for place in range(fold):
                piece = canvas[group * fold + place, 0:tall, base : base + lanes]
                turn = (place * cols - at) % lanes
                if turn:
                    piece = pltpu.roll(piece, turn, 1)
                packed = piece if packed is None else jnp.where(lane == place, piece, packed)
            block[owner, group * rows : (group + 1) * rows, :] = packed[radius : radius + rows]
            at_rim = pl.ds(group * radius, radius)
            rim[0, owner, at_rim, :] = packed[:radius]
            rim[1, owner, at_rim, :] = packed[tall - radius :]

    def edge(down, slot, peer):
        return pltpu.make_async_remote_copy(
            src_ref=rim.at[int(down), peer],
            dst_ref=rim_in.at[int(down), slot],
            send_sem=rim_send.at[int(down), slot],
            recv_sem=rim_recv.at[int(down), slot],
            device_id={"samp": peer, "band": here + 1 if down else here - 1},
            device_id_type=MESH,
        )

    @pl.when(has_below)
    def _():
        for slot, peer in enumerate([me] + peers):
            edge(True, slot, peer).start()

    @pl.when(has_above)
    def _():
        for slot, peer in enumerate([me] + peers):
            edge(False, slot, peer).start()

    splats = []
    for slot, peer in enumerate(peers):
        copy = pltpu.make_async_remote_copy(
            src_ref=block.at[peer],
            dst_ref=block_in.at[slot],
            send_sem=cs_send.at[slot],
            recv_sem=cs_recv.at[slot],
            device_id={"samp": peer},
            device_id_type=MESH,
        )
        copy.start()
        splats.append(copy)
    for copy in sums + gathers:
        copy.wait_send()

    @pl.when(has_below)
    def _():
        halo(True).wait_send()

    @pl.when(has_above)
    def _():
        halo(False).wait_send()

    @pl.when(here == 0)
    def _():
        rim_in[1] = jnp.zeros(rim_in.shape[1:], jnp.float32)

    @pl.when(here == bands - 1)
    def _():
        rim_in[0] = jnp.zeros(rim_in.shape[1:], jnp.float32)

    total = block[me]
    for slot, copy in enumerate(splats):
        copy.wait_recv()
        total = total + block_in[slot]

    @pl.when(has_above)
    def _():
        for slot, peer in enumerate([me] + peers):
            edge(True, slot, peer).wait_recv()

    @pl.when(has_below)
    def _():
        for slot, peer in enumerate([me] + peers):
            edge(False, slot, peer).wait_recv()

    below = rim_in[0, 0]
    above = rim_in[1, 0]
    for slot in range(1, count):
        below = below + rim_in[0, slot]
        above = above + rim_in[1, slot]

    planes = []
    for group in range(groups):
        near = slice(group * radius, (group + 1) * radius)
        gap = jnp.zeros((rows - 2 * radius, lanes), jnp.float32)
        body = total[group * rows : (group + 1) * rows]
        body = body + jnp.concatenate([above[near], gap, below[near]], axis=0)
        for place in range(fold):
            planes.append(pltpu.roll(body, lanes - place * cols, 1) if place else body)
    for chan in range(3):
        out_ref[chan] = (planes[chan] / planes[3])[:, :cols]
    for copy in splats:
        copy.wait_send()

    @pl.when(has_below)
    def _():
        for slot, peer in enumerate([me] + peers):
            edge(True, slot, peer).wait_send()

    @pl.when(has_above)
    def _():
        for slot, peer in enumerate([me] + peers):
            edge(False, slot, peer).wait_send()


def fits(features, third, count):
    _, samples_dev, rows, width = features.shape
    radius = KSIZE // 2
    lanes = LANES
    cols = width // count
    return (
        samples_dev == 1
        and count > 1
        and rows % count == 0
        and rows % 8 == 0
        and rows >= 2 * radius
        and width % lanes == 0
        and lanes % cols == 0
        and lanes // cols in (1, 2, 4)
        and third.shape[0] % 16 == 0
    )


def fused_shards(
    features,
    radiance,
    sample_order,
    embed_first,
    embed_second,
    embed_third,
    conv_first,
    conv_second,
    kernel_first,
    kernel_second,
):
    count = lax.axis_size("samp")
    bands = lax.axis_size("band")
    channels, samples_dev, rows, width = features.shape
    emb_width = embed_third.shape[0]
    radius = KSIZE // 2
    tall = rows + 2 * radius
    cols = width // count
    groups = 4 * cols // LANES
    taps_pad = -(-KSIZE * KSIZE // 8) * 8
    scaling = 1.0 / math.sqrt(samples_dev * count)
    vmem = pl.BlockSpec(memory_space=pltpu.VMEM)
    operands = (
        features,
        radiance,
        jnp.swapaxes(sample_order, 2, 3),
        embed_first.T,
        embed_second,
        embed_third,
        conv_first.T,
        conv_second,
        kernel_first.T,
        kernel_second,
    )
    sem = pltpu.SemaphoreType.DMA
    rim_rows = -(-groups * radius // 8) * 8
    return pl.pallas_call(
        functools.partial(staged, count, bands, scaling),
        out_shape=jax.ShapeDtypeStruct((3, rows, cols), jnp.float32),
        in_specs=[pl.BlockSpec(memory_space=pl.ANY)] * len(operands),
        out_specs=vmem,
        scratch_shapes=[
            pltpu.VMEM(embed_first.shape, jnp.bfloat16),
            pltpu.VMEM(conv_first.shape, jnp.bfloat16),
            pltpu.VMEM(kernel_first.shape, jnp.bfloat16),
            pltpu.VMEM((width // LANES, channels * rows, LANES), jnp.float32),
            pltpu.VMEM((3, rows, width), jnp.float32),
            pltpu.VMEM((rows, emb_width, width), jnp.bfloat16),
            pltpu.VMEM((count - 1, rows // count, emb_width, width), SENT),
            pltpu.VMEM((count - 1, rows // count, emb_width, width), SENT),
            pltpu.VMEM((tall, emb_width, width), jnp.bfloat16),
            pltpu.VMEM((tall * KSIZE * emb_width, width), jnp.bfloat16),
            pltpu.VMEM((width // LANES, rows * taps_pad, LANES), jnp.float32),
            pltpu.VMEM((4, -(-tall // 8) * 8, width), jnp.float32),
            pltpu.VMEM((count, groups * rows, LANES), jnp.float32),
            pltpu.VMEM((count - 1, groups * rows, LANES), jnp.float32),
            pltpu.VMEM((2, count, rim_rows, LANES), jnp.float32),
            pltpu.VMEM((2, count, rim_rows, LANES), jnp.float32),
            sem((count - 1, rows // count)),
            sem((count - 1, rows // count)),
            sem((count - 1, rows // count)),
            sem((count, rows // count)),
            sem((2,)),
            sem((2,)),
            sem((count - 1,)),
            sem((count - 1,)),
            sem((2, count)),
            sem((2, count)),
            *[pltpu.VMEM(value.shape, value.dtype) for value in operands],
            sem((len(operands),)),
        ],
        compiler_params=pltpu.CompilerParams(collective_id=0, has_side_effects=True),
    )(*operands)


def either(*operands):
    if fits(operands[0], operands[5], lax.axis_size("samp")):
        return fused_shards(*operands)
    return shards(*operands)


def solution(mesh):
    in_specs = (
        P(None, ("group", "samp"), "band", None),
        P(None, ("group", "samp"), "band", None),
        P(("group", "samp"), "band", None, None),
        P(),
        P(),
        P(),
        P(),
        P(),
        P(),
        P(),
    )
    out_specs = P(None, ("group", "band"), "samp")
    return jax.shard_map(either, mesh=mesh, in_specs=in_specs, out_specs=out_specs, check_vma=False)
```

```python
import functools
import math

import jax
import jax.numpy as jnp
from jax import lax
from jax.experimental import pallas as pl
from jax.experimental.pallas import tpu as pltpu
from jax.sharding import PartitionSpec as P

KSIZE = 5
LANES = 128
SENT = jnp.float32


def padded_2(cells, sides, width):
    for axis, dim in sides:
        count = lax.axis_size(axis)
        ends = count - 1
        head = lax.slice_in_dim(cells, 0, width, axis=dim)
        tail = lax.slice_in_dim(cells, cells.shape[dim] - width, cells.shape[dim], axis=dim)
        cells = jnp.concatenate(
            [
                lax.ppermute(tail, axis, [(i, (i + 1) % count) for i in range(ends)]),
                cells,
                lax.ppermute(head, axis, [((i + 1) % count, i) for i in range(ends)]),
            ],
            axis=dim,
        )
    return cells


def passed_along(block, axis, distance):
    devices = range(lax.axis_size(axis))
    route = [(i - distance, i) for i in devices if i - distance in devices]
    return lax.ppermute(block, axis, route)


def to_pixels(values, sample_order):
    tile_size = sample_order.shape[-1]
    dest_cols = sample_order.reshape(sample_order.shape[:-2] + (-1,))
    offsets = jnp.arange(dest_cols.shape[-1], dtype=jnp.int32) % tile_size
    result = jnp.zeros_like(values)
    for slot_id in range(tile_size):
        spread = jnp.repeat(values[..., slot_id::tile_size], tile_size, axis=-1)
        target = jnp.repeat(dest_cols[..., slot_id::tile_size], tile_size, axis=-1)
        result = jnp.where((target == offsets)[None], spread, result)
    return result


def embed_samples(columns, embed_first, embed_second, embed_third):
    layer_one = jax.nn.relu(
        jnp.dot(embed_first, columns, preferred_element_type=jnp.float32)
    ).astype(jnp.bfloat16)
    layer_two = jax.nn.relu(
        jnp.dot(embed_second, layer_one, preferred_element_type=jnp.float32)
    ).astype(jnp.bfloat16)
    return jnp.dot(embed_third, layer_two, preferred_element_type=jnp.float32)


def convolve(padded, row_count, col_count, conv_first, conv_second):
    shifted = [
        padded[:, row_off : row_off + row_count, col_off : col_off + col_count]
        for row_off in range(KSIZE)
        for col_off in range(KSIZE)
    ]
    stacked = jnp.stack(shifted).reshape(-1, row_count * col_count)
    hidden = jax.nn.relu(jnp.dot(conv_first, stacked, preferred_element_type=jnp.float32)).astype(
        jnp.bfloat16
    )
    result = jnp.dot(conv_second, hidden, preferred_element_type=jnp.float32).astype(jnp.bfloat16)
    return result.reshape(-1, row_count, col_count)


def shards(
    features,
    radiance,
    sample_order,
    embed_first,
    embed_second,
    embed_third,
    conv_first,
    conv_second,
    kernel_first,
    kernel_second,
):
    ordered = to_pixels(features, sample_order)
    lights = to_pixels(radiance, sample_order)
    channels, samples_dev, row_count, crop_width = ordered.shape
    emb_width = embed_third.shape[0]
    radius = KSIZE // 2
    scaling = 1.0 / math.sqrt(samples_dev * lax.axis_size("samp"))
    embedded = embed_samples(ordered.reshape(channels, -1), embed_first, embed_second, embed_third)
    emb_bf = embedded.astype(jnp.bfloat16)
    own_part = jnp.dot(kernel_first[:, :emb_width], emb_bf, preferred_element_type=jnp.float32)
    own_part = own_part.reshape(-1, samples_dev, row_count, crop_width)
    partial_value = jnp.sum(embedded.reshape(emb_width, samples_dev, row_count, crop_width), axis=1)
    summed_emb = lax.psum(partial_value, "samp")
    pooled = (summed_emb * scaling).astype(jnp.bfloat16)
    padded = padded_2(pooled, (("band", 1),), 2)
    padded = jnp.pad(padded, ((0, 0), (0, 0), (radius, radius)))
    context = convolve(padded, row_count, crop_width, conv_first, conv_second)
    col_count = context.shape[2]
    ctx_part = jnp.dot(
        kernel_first[:, emb_width:],
        context.reshape(emb_width, -1),
        preferred_element_type=jnp.float32,
    )
    ctx_part = ctx_part.reshape(-1, 1, row_count, col_count)
    hidden = jax.nn.relu(own_part + ctx_part).astype(jnp.bfloat16)
    logits = jnp.dot(
        kernel_second, hidden.reshape(hidden.shape[0], -1), preferred_element_type=jnp.float32
    )
    weights = jnp.exp(logits).reshape(-1, samples_dev, row_count, col_count)
    with_ones = jnp.concatenate(
        [lights, jnp.ones((1, samples_dev, row_count, crop_width), jnp.float32)], axis=0
    )
    canvas = jnp.zeros((4, row_count + 2 * radius, crop_width + 2 * radius), jnp.float32)
    for row_off in range(KSIZE):
        for col_off in range(KSIZE):
            tap_index = row_off * KSIZE + col_off
            contrib = jnp.sum(weights[tap_index][None] * with_ones, axis=1)
            canvas = canvas.at[
                :, row_off : row_off + row_count, col_off : col_off + crop_width
            ].add(contrib)
    canvas = canvas[:, :, radius : radius + crop_width]
    summed_all = lax.psum_scatter(canvas, "samp", scatter_dimension=2, tiled=True)
    top_rims = summed_all[:, :radius]
    low_rims = summed_all[:, radius + row_count :]
    summed = summed_all[:, radius : radius + row_count]
    from_below = passed_along(top_rims, "band", -1)
    from_above = passed_along(low_rims, "band", 1)
    summed = summed.at[:, row_count - radius :].add(from_below)
    summed = summed.at[:, :radius].add(from_above)
    return summed[:3] / summed[3:4]


MESH = pl.DeviceIdType.MESH


def slots_to_sources(order, width):
    rows, tile_size, tiles = order.shape
    flat = order.reshape(rows * tile_size, tiles).astype(jnp.float32).astype(jnp.bfloat16)
    tile = lax.broadcasted_iota(jnp.int32, (tiles, width), 0)
    col = lax.broadcasted_iota(jnp.int32, (tiles, width), 1)
    spread = jnp.where(tile == col // tile_size, 1.0, 0.0).astype(jnp.bfloat16)
    wide = jnp.dot(flat, spread, preferred_element_type=jnp.float32).astype(jnp.int32)
    slot = lax.broadcasted_iota(jnp.int32, (rows * tile_size, width), 0) % tile_size
    offset = lax.broadcasted_iota(jnp.int32, (rows * tile_size, width), 1) % tile_size
    wide = jnp.where(wide == offset, slot, 0)
    slots = jnp.sum(wide.reshape(rows, tile_size, width), axis=1)
    col = lax.broadcasted_iota(jnp.int32, (rows, width), 1)
    return col // tile_size * tile_size + slots


def share_of(device, count):
    if count % 2:
        return device
    return device + 1 - 2 * (device % 2)


def staged(count, bands, scaling, *refs):
    sources, held, load_sem = refs[:10], refs[-11:-1], refs[-1]
    loads = [
        pltpu.make_async_copy(source, target, load_sem.at[place])
        for place, (source, target) in enumerate(zip(sources, held))
    ]
    fused(count, bands, scaling, loads, *held, *refs[10:-11])


def fused(
    count,
    bands,
    scaling,
    loads,
    feat_ref,
    rad_ref,
    order_ref,
    first_turned,
    second_ref,
    third_ref,
    conv_one_turned,
    conv_two_ref,
    kern_one_turned,
    kern_two_ref,
    out_ref,
    first_ref,
    conv_one_ref,
    kern_one_ref,
    plane,
    light,
    emb_bf,
    part,
    part_in,
    pooled,
    taps,
    logit,
    canvas,
    block,
    block_in,
    rim,
    rim_in,
    rs_send,
    rs_recv,
    ag_send,
    ag_recv,
    halo_send,
    halo_recv,
    cs_send,
    cs_recv,
    rim_send,
    rim_recv,
):
    channels, _, rows, width = feat_ref.shape
    emb_width = third_ref.shape[0]
    radius = KSIZE // 2
    share = rows // count
    tall = rows + 2 * radius
    cols = width // count
    lanes = block.shape[-1]
    fold = lanes // cols
    groups = 4 // fold
    me = lax.axis_index("samp")
    here = lax.axis_index("band")
    peers = [lax.rem(me + step, count) for step in range(1, count)]
    chunk = share_of(me, count)
    has_above = here > 0
    has_below = here < bands - 1

    barrier = pltpu.get_barrier_semaphore()
    for peer in peers:
        pl.semaphore_signal(barrier, inc=1, device_id={"samp": peer}, device_id_type=MESH)

    @pl.when(has_above)
    def _():
        pl.semaphore_signal(barrier, inc=1, device_id={"band": here - 1}, device_id_type=MESH)

    @pl.when(has_below)
    def _():
        pl.semaphore_signal(barrier, inc=1, device_id={"band": here + 1}, device_id_type=MESH)

    for place in (2, 0, 3, 4, 5, 1, 6, 8, 7, 9):
        loads[place].start()

    loads[2].wait()
    source = slots_to_sources(order_ref[0], width)
    halves = []
    for start in range(0, width, lanes):
        halves.append((start, source[:, start : start + lanes] - start))

    def reorder(values):
        return [
            jnp.take_along_axis(
                values[:, start : start + lanes], index, axis=1, mode="promise_in_bounds"
            )
            for start, index in halves
        ]

    def strided(ref, start, size, stride):
        return jnp.concatenate(
            [ref[half, pl.ds(start, size, stride=stride), :] for half in range(ref.shape[0])],
            axis=1,
        )

    loads[0].wait()
    for chan in range(channels):
        for half, part_x in enumerate(reorder(feat_ref[chan, 0].astype(jnp.float32))):
            plane[half, chan * rows : (chan + 1) * rows, :] = part_x

    for place in (3, 4, 5):
        loads[place].wait()
    first_ref[...] = first_turned[...].T

    def embed_row(row):
        x = strided(plane, row, channels, rows).astype(jnp.bfloat16)
        x = jnp.dot(first_ref[...], x, preferred_element_type=jnp.float32)
        x = jnp.maximum(x, 0.0).astype(jnp.bfloat16)
        x = jnp.dot(second_ref[...], x, preferred_element_type=jnp.float32)
        x = jnp.maximum(x, 0.0).astype(jnp.bfloat16)
        x = jnp.dot(third_ref[...], x, preferred_element_type=jnp.float32)
        emb_bf[row] = x.astype(jnp.bfloat16)
        return x

    beside = jnp.minimum(here, 1) + jnp.minimum(bands - 1 - here, 1)
    sums = []
    for row in range(share):
        for slot, peer in enumerate(peers):
            part[slot, row] = embed_row(share_of(peer, count) * share + row).astype(part.dtype)
            if not sums:
                pl.semaphore_wait(barrier, count - 1 + beside)
            copy = pltpu.make_async_remote_copy(
                src_ref=part.at[slot, row],
                dst_ref=part_in.at[slot, row],
                send_sem=rs_send.at[slot, row],
                recv_sem=rs_recv.at[slot, row],
                device_id={"samp": peer},
                device_id_type=MESH,
            )
            copy.start()
            sums.append(copy)
    total = [embed_row(chunk * share + row) for row in range(share)]
    loads[1].wait()
    for chan in range(3):
        light[chan] = jnp.concatenate(reorder(rad_ref[chan, 0]), axis=1)
    for place in (6, 8, 7, 9):
        loads[place].wait()
    conv_one_ref[...] = conv_one_turned[...].T
    kern_one_ref[...] = kern_one_turned[...].T
    canvas[...] = jnp.zeros(canvas.shape, jnp.float32)

    def gather(slot, row, peer, sender):
        at = radius + share_of(sender, count) * share + row
        return pltpu.make_async_remote_copy(
            src_ref=pooled.at[at],
            dst_ref=pooled.at[at],
            send_sem=ag_send.at[slot, row],
            recv_sem=ag_recv.at[sender, row],
            device_id={"samp": peer},
            device_id_type=MESH,
        )

    gathers = []
    for row in range(share):
        summed = total[row]
        for slot in range(count - 1):
            sums[row * (count - 1) + slot].wait_recv()
            summed = summed + part_in[slot, row].astype(jnp.float32)
        pooled[radius + chunk * share + row] = (summed * scaling).astype(jnp.bfloat16)
        for slot, peer in enumerate(peers):
            copy = gather(slot, row, peer, me)
            copy.start()
            gathers.append(copy)

    def halo(down):
        start = rows if down else radius
        goal = 0 if down else rows + radius
        return pltpu.make_async_remote_copy(
            src_ref=pooled.at[pl.ds(start, radius)],
            dst_ref=pooled.at[pl.ds(goal, radius)],
            send_sem=halo_send.at[int(down)],
            recv_sem=halo_recv.at[int(down)],
            device_id={"band": here + 1 if down else here - 1},
            device_id_type=MESH,
        )

    @pl.when(here == 0)
    def _():
        pooled[0:radius] = jnp.zeros((radius, emb_width, width), jnp.bfloat16)

    @pl.when(here == bands - 1)
    def _():
        pooled[rows + radius : tall] = jnp.zeros((radius, emb_width, width), jnp.bfloat16)

    depth = KSIZE * emb_width
    col = lax.broadcasted_iota(jnp.int32, (emb_width, width), 1)

    def spread_row(row):
        values = pooled[row].astype(jnp.float32)
        for col_off in range(KSIZE):
            shift = col_off - radius
            if shift == 0:
                moved = values
            else:
                moved = pltpu.roll(values, (-shift) % width, 1)
                moved = jnp.where((col + shift >= 0) & (col + shift < width), moved, 0.0)
            start = row * depth + col_off * emb_width
            taps[start : start + emb_width, :] = moved.astype(jnp.bfloat16)

    def weigh_row(row):
        stacked = taps[row * depth : row * depth + KSIZE * depth, :]
        hidden = jnp.dot(conv_one_ref[...], stacked, preferred_element_type=jnp.float32)
        hidden = jnp.maximum(hidden, 0.0).astype(jnp.bfloat16)
        context = jnp.dot(conv_two_ref[...], hidden, preferred_element_type=jnp.float32)
        both = jnp.concatenate([emb_bf[row], context.astype(jnp.bfloat16)], axis=0)
        hidden = jnp.dot(kern_one_ref[...], both, preferred_element_type=jnp.float32)
        hidden = jnp.maximum(hidden, 0.0).astype(jnp.bfloat16)
        start = row * (logit.shape[1] // rows)
        values = jnp.dot(kern_two_ref[...], hidden, preferred_element_type=jnp.float32)
        for half in range(logit.shape[0]):
            logit[half, start : start + KSIZE * KSIZE, :] = values[
                :, half * lanes : (half + 1) * lanes
            ]

    edges = -(-radius // share)
    order = list(range(edges)) + list(range(count - edges, count))
    order = list(dict.fromkeys(order))
    order += [share_id for share_id in range(count) if share_id not in order]
    for place, share_id in enumerate(order):
        owner = share_of(share_id, count)

        @pl.when(me != owner)
        def _():
            for row in range(share):
                gather(0, row, peers[0], owner).wait_recv()

        if place == edges - 1:

            @pl.when(has_above)
            def _():
                halo(False).start()

        if place == min(2 * edges, count) - 1:

            @pl.when(has_below)
            def _():
                halo(True).start()

        if place >= min(2 * edges, count) - 1:
            ready = order[: place + 1] if place == min(2 * edges, count) - 1 else [share_id]
            for done in ready:
                for row in range(share):
                    spread_row(radius + done * share + row)
    inner = range(radius, rows - radius)
    for row in inner:
        weigh_row(row)

    @pl.when(has_above)
    def _():
        halo(True).wait_recv()

    @pl.when(has_below)
    def _():
        halo(False).wait_recv()

    for row in range(tall):
        if row < radius or row >= rows + radius:
            spread_row(row)
    for row in range(rows):
        if row not in inner:
            weigh_row(row)

    col = lax.broadcasted_iota(jnp.int32, (rows, width), 1)
    colours = [light[chan] for chan in range(3)]
    stride = logit.shape[1] // rows
    for row_off in range(KSIZE):
        sums_c = [None] * 4
        for col_off in range(KSIZE):
            shift = col_off - radius
            weight = jnp.exp(strided(logit, row_off * KSIZE + col_off, rows, stride))
            if shift != 0:
                weight = jnp.where((col + shift >= 0) & (col + shift < width), weight, 0.0)
            for chan in range(4):
                term = weight * colours[chan] if chan < 3 else weight
                if shift != 0:
                    term = pltpu.roll(term, shift % width, 1)
                sums_c[chan] = term if sums_c[chan] is None else sums_c[chan] + term
        for chan in range(4):
            canvas[chan, row_off : row_off + rows, :] += sums_c[chan]

    lane = lax.broadcasted_iota(jnp.int32, (tall, lanes), 1) // cols
    for owner in range(count):
        base = owner * cols // lanes * lanes
        at = owner * cols - base
        for group in range(groups):
            packed = None
            for place in range(fold):
                piece = canvas[group * fold + place, 0:tall, base : base + lanes]
                turn = (place * cols - at) % lanes
                if turn:
                    piece = pltpu.roll(piece, turn, 1)
                packed = piece if packed is None else jnp.where(lane == place, piece, packed)
            block[owner, group * rows : (group + 1) * rows, :] = packed[radius : radius + rows]
            at_rim = pl.ds(group * radius, radius)
            rim[0, owner, at_rim, :] = packed[:radius]
            rim[1, owner, at_rim, :] = packed[tall - radius :]

    def edge(down, slot, peer):
        return pltpu.make_async_remote_copy(
            src_ref=rim.at[int(down), peer],
            dst_ref=rim_in.at[int(down), slot],
            send_sem=rim_send.at[int(down), slot],
            recv_sem=rim_recv.at[int(down), slot],
            device_id={"samp": peer, "band": here + 1 if down else here - 1},
            device_id_type=MESH,
        )

    @pl.when(has_below)
    def _():
        for slot, peer in enumerate([me] + peers):
            edge(True, slot, peer).start()

    @pl.when(has_above)
    def _():
        for slot, peer in enumerate([me] + peers):
            edge(False, slot, peer).start()

    splats = []
    for slot, peer in enumerate(peers):
        copy = pltpu.make_async_remote_copy(
            src_ref=block.at[peer],
            dst_ref=block_in.at[slot],
            send_sem=cs_send.at[slot],
            recv_sem=cs_recv.at[slot],
            device_id={"samp": peer},
            device_id_type=MESH,
        )
        copy.start()
        splats.append(copy)
    for copy in sums + gathers:
        copy.wait_send()

    @pl.when(has_below)
    def _():
        halo(True).wait_send()

    @pl.when(has_above)
    def _():
        halo(False).wait_send()

    @pl.when(here == 0)
    def _():
        rim_in[1] = jnp.zeros(rim_in.shape[1:], jnp.float32)

    @pl.when(here == bands - 1)
    def _():
        rim_in[0] = jnp.zeros(rim_in.shape[1:], jnp.float32)

    total = block[me]
    for slot, copy in enumerate(splats):
        copy.wait_recv()
        total = total + block_in[slot]

    @pl.when(has_above)
    def _():
        for slot, peer in enumerate([me] + peers):
            edge(True, slot, peer).wait_recv()

    @pl.when(has_below)
    def _():
        for slot, peer in enumerate([me] + peers):
            edge(False, slot, peer).wait_recv()

    below = rim_in[0, 0]
    above = rim_in[1, 0]
    for slot in range(1, count):
        below = below + rim_in[0, slot]
        above = above + rim_in[1, slot]

    planes = []
    for group in range(groups):
        near = slice(group * radius, (group + 1) * radius)
        gap = jnp.zeros((rows - 2 * radius, lanes), jnp.float32)
        body = total[group * rows : (group + 1) * rows]
        body = body + jnp.concatenate([above[near], gap, below[near]], axis=0)
        for place in range(fold):
            planes.append(pltpu.roll(body, lanes - place * cols, 1) if place else body)
    for chan in range(3):
        out_ref[chan] = (planes[chan] / planes[3])[:, :cols]
    for copy in splats:
        copy.wait_send()

    @pl.when(has_below)
    def _():
        for slot, peer in enumerate([me] + peers):
            edge(True, slot, peer).wait_send()

    @pl.when(has_above)
    def _():
        for slot, peer in enumerate([me] + peers):
            edge(False, slot, peer).wait_send()


def fits(features, third, count):
    _, samples_dev, rows, width = features.shape
    radius = KSIZE // 2
    lanes = LANES
    cols = width // count
    return (
        samples_dev == 1
        and count > 1
        and rows % count == 0
        and rows % 8 == 0
        and rows >= 2 * radius
        and width % lanes == 0
        and lanes % cols == 0
        and lanes // cols in (1, 2, 4)
        and third.shape[0] % 16 == 0
    )


def fused_shards(
    features,
    radiance,
    sample_order,
    embed_first,
    embed_second,
    embed_third,
    conv_first,
    conv_second,
    kernel_first,
    kernel_second,
):
    count = lax.axis_size("samp")
    bands = lax.axis_size("band")
    channels, samples_dev, rows, width = features.shape
    emb_width = embed_third.shape[0]
    radius = KSIZE // 2
    tall = rows + 2 * radius
    cols = width // count
    groups = 4 * cols // LANES
    taps_pad = -(-KSIZE * KSIZE // 8) * 8
    scaling = 1.0 / math.sqrt(samples_dev * count)
    vmem = pl.BlockSpec(memory_space=pltpu.VMEM)
    operands = (
        features,
        radiance,
        jnp.swapaxes(sample_order, 2, 3),
        embed_first.T,
        embed_second,
        embed_third,
        conv_first.T,
        conv_second,
        kernel_first.T,
        kernel_second,
    )
    sem = pltpu.SemaphoreType.DMA
    rim_rows = -(-groups * radius // 8) * 8
    return pl.pallas_call(
        functools.partial(staged, count, bands, scaling),
        out_shape=jax.ShapeDtypeStruct((3, rows, cols), jnp.float32),
        in_specs=[pl.BlockSpec(memory_space=pl.ANY)] * len(operands),
        out_specs=vmem,
        scratch_shapes=[
            pltpu.VMEM(embed_first.shape, jnp.bfloat16),
            pltpu.VMEM(conv_first.shape, jnp.bfloat16),
            pltpu.VMEM(kernel_first.shape, jnp.bfloat16),
            pltpu.VMEM((width // LANES, channels * rows, LANES), jnp.float32),
            pltpu.VMEM((3, rows, width), jnp.float32),
            pltpu.VMEM((rows, emb_width, width), jnp.bfloat16),
            pltpu.VMEM((count - 1, rows // count, emb_width, width), SENT),
            pltpu.VMEM((count - 1, rows // count, emb_width, width), SENT),
            pltpu.VMEM((tall, emb_width, width), jnp.bfloat16),
            pltpu.VMEM((tall * KSIZE * emb_width, width), jnp.bfloat16),
            pltpu.VMEM((width // LANES, rows * taps_pad, LANES), jnp.float32),
            pltpu.VMEM((4, -(-tall // 8) * 8, width), jnp.float32),
            pltpu.VMEM((count, groups * rows, LANES), jnp.float32),
            pltpu.VMEM((count - 1, groups * rows, LANES), jnp.float32),
            pltpu.VMEM((2, count, rim_rows, LANES), jnp.float32),
            pltpu.VMEM((2, count, rim_rows, LANES), jnp.float32),
            sem((count - 1, rows // count)),
            sem((count - 1, rows // count)),
            sem((count - 1, rows // count)),
            sem((count, rows // count)),
            sem((2,)),
            sem((2,)),
            sem((count - 1,)),
            sem((count - 1,)),
            sem((2, count)),
            sem((2, count)),
            *[pltpu.VMEM(value.shape, value.dtype) for value in operands],
            sem((len(operands),)),
        ],
        compiler_params=pltpu.CompilerParams(collective_id=0, has_side_effects=True),
    )(*operands)


def either(*operands):
    if fits(operands[0], operands[5], lax.axis_size("samp")):
        return fused_shards(*operands)
    return shards(*operands)


def solution(mesh):
    in_specs = (
        P(None, ("group", "samp"), "band", None),
        P(None, ("group", "samp"), "band", None),
        P(("group", "samp"), "band", None, None),
        P(),
        P(),
        P(),
        P(),
        P(),
        P(),
        P(),
    )
    out_specs = P(None, ("group", "band"), "samp")
    return jax.shard_map(either, mesh=mesh, in_specs=in_specs, out_specs=out_specs, check_vma=False)
```
